128 devices in a mesh: leaf: 16 (over x, y), side: 8 (over z, core).
Axes of the slice: x: 4, y: 4, z: 4, core: 2. Of those that a mesh axis runs over, the one named last changes fastest.
Arguments:
- block: float32 [131072, 512], P(('leaf', 'side')), may hold values from -24 to 24
- basis: float32 [131072, 1024], P(('leaf', 'side')), may hold values from -1 to 1
Outputs:
- ortho: float32 [131072, 512], P(('leaf', 'side'))
- factor: float32 [512, 512], replicated
- coeffs: float32 [1024, 512], replicated
The draws below stay inside these ranges and needn't reach their ends.
All inputs are finite; a program needn't handle non-finite values.
Results may differ from the reference program's by a relative error of at most 0.0001.
Values sent between devices are 32-bit elements; how exact they have to be, the bound alone decides.
A program may use at most 64 MiB of HBM per device.

```python
import math
import jax
import jax.numpy as jnp
from jax import lax

K = 512
P_SIZE = 1024
ROWS = 131072


def basis_of(key):
    raw_normal = jax.random.normal(jax.random.fold_in(key, 101), (ROWS, P_SIZE), jnp.float32)
    return jnp.clip(raw_normal, -6.0, 6.0) * (1.0 / math.sqrt(ROWS))


def draw_basis(key, part):
    return basis_of(key)


def draw_block(key, part):
    basis = basis_of(key)
    key_core, key_rows, key_cols, key_left, key_size, key_sign = jax.random.split(jax.random.fold_in(key, 202), 6)
    core_draw = jax.random.normal(key_core, (ROWS, K), jnp.float32)
    log_span = math.log(10.0)
    row_power = (math.exp(2.0 * log_span) - 1.0) / (2.0 * log_span) * 2.0
    row_ramp = jnp.sqrt(1.0 + 2.0 * jnp.arange(ROWS, dtype=jnp.float32) / ROWS)
    row_scale = jnp.exp(jax.random.uniform(key_rows, (ROWS, 1), jnp.float32) * log_span) * row_ramp[:, None]
    col_scale = jnp.exp(jax.random.uniform(key_cols, (1, K), jnp.float32) * math.log(3.0))
    fresh = core_draw * row_scale * col_scale
    mixing = 32
    mix_left = jax.random.normal(key_left, (P_SIZE, mixing), jnp.float32) * (1.0 / math.sqrt(mixing))
    magnitude = jax.random.uniform(key_size, (K, mixing), jnp.float32, 0.8, 1.2)
    mix_right = magnitude * jnp.sign(jax.random.normal(key_sign, (K, mixing), jnp.float32))
    lifted = jnp.dot(basis, mix_left, precision=lax.Precision.HIGHEST, preferred_element_type=jnp.float32)
    spanned = jnp.dot(lifted, mix_right.T, precision=lax.Precision.HIGHEST, preferred_element_type=jnp.float32)
    spanned = spanned * col_scale * math.sqrt(ROWS * row_power / P_SIZE)
    return jnp.clip(0.04 * (fresh + spanned), -24.0, 24.0)


def setup_inputs(seed: int = 0) -> dict:
    seeds = jax.random.split(jax.random.key(seed), 3)
    block = draw_block(jax.random.fold_in(seeds[2], 71), 0)
    basis = draw_basis(jax.random.fold_in(seeds[2], 71), 0)
    return {"block": block, "basis": basis}


def inner(left, right):
    return lax.dot_general(left, right, (((0,), (0,)), ((), ())), precision=lax.Precision.HIGHEST, preferred_element_type=jnp.float32)

def product(left, right):
    return jnp.dot(left, right, precision=lax.Precision.HIGHEST, preferred_element_type=jnp.float32)

def small_upper(matrix):
    width = matrix.shape[0]
    positions = jnp.arange(width, dtype=jnp.int32)

    def one_step(column, carry):
        rest, result = carry
        column = jnp.asarray(column).astype(jnp.int32)
        row = lax.dynamic_slice_in_dim(rest, column, 1, 0)[0]
        pivot = jnp.sqrt(jnp.sum(jnp.where(positions == column, row, jnp.float32(0.0))))
        new_row = jnp.where(positions >= column, row / pivot, jnp.float32(0.0))
        result = lax.dynamic_update_slice_in_dim(result, new_row[None, :], column, 0)
        rest = rest - new_row[:, None] * new_row[None, :]
        return (rest, result)
    start = (matrix, jnp.zeros_like(matrix))
    return lax.fori_loop(0, width, one_step, start)[1]

def small_inverse(upper_block):
    width = upper_block.shape[0]
    positions = jnp.arange(width, dtype=jnp.int32)

    def one_step(count, result):
        index = (width - 1 - jnp.asarray(count)).astype(jnp.int32)
        row = lax.dynamic_slice_in_dim(upper_block, index, 1, 0)[0]
        pivot = jnp.sum(jnp.where(positions == index, row, jnp.float32(0.0)))
        beyond = jnp.where(positions > index, row, jnp.float32(0.0))
        unit = jnp.where(positions == index, jnp.float32(1.0), jnp.float32(0.0))
        new_row = (unit - product(beyond[None, :], result)[0]) / pivot
        return lax.dynamic_update_slice_in_dim(result, new_row[None, :], index, 0)
    return lax.fori_loop(0, width, one_step, jnp.zeros_like(upper_block))

def factor_and_inverse(gram):
    width = gram.shape[0]
    piece = min(128, width)
    count = width // piece
    rest = gram
    strips = []
    diag_inverses = []
    for index in range(count):
        diag = small_upper(rest[:piece, :piece])
        diag_inv = small_inverse(diag)
        right = product(diag_inv.T, rest[:piece, piece:])
        left_zeros = jnp.zeros((piece, index * piece), gram.dtype)
        strips.append(jnp.concatenate([left_zeros, diag, right], axis=1))
        diag_inverses.append(diag_inv)
        rest = rest[piece:, piece:] - inner(right, right)
    factor = jnp.concatenate(strips, axis=0)
    lower_part = None
    for index in reversed(range(count)):
        diag_inv = diag_inverses[index]
        left_zeros = jnp.zeros((piece, index * piece), gram.dtype)
        if lower_part is None:
            strip = jnp.concatenate([left_zeros, diag_inv], axis=1)
            lower_part = diag_inv
        else:
            coupling = factor[index * piece:(index + 1) * piece, (index + 1) * piece:]
            far = -product(diag_inv, product(coupling, lower_part))
            top = jnp.concatenate([diag_inv, far], axis=1)
            below = jnp.concatenate([jnp.zeros((lower_part.shape[0], piece), gram.dtype), lower_part], axis=1)
            lower_part = jnp.concatenate([top, below], axis=0)
    return (factor, lower_part)

def reference(block, basis):
    coeffs = inner(basis, block)
    projected = block - product(basis, coeffs)
    gram = inner(projected, projected) / ROWS
    factor, inverse = factor_and_inverse(gram)
    ortho = product(projected, inverse)
    return (ortho, factor, coeffs)
```

```python
import functools
import jax
import jax.numpy as jnp
from jax import lax
from jax.experimental import pallas as pl
from jax.experimental.pallas import tpu as pltpu
from jax.sharding import PartitionSpec as P

F32 = jnp.float32
BF16 = jnp.bfloat16
MESH = pl.DeviceIdType.MESH
HI = lax.Precision.HIGHEST
AXES = ((0, 1, 2), (1, 2, 0), (2, 0, 1))


def position():
    leaf, side = lax.axis_index("leaf"), lax.axis_index("side")
    return [leaf // 4, lax.rem(leaf, 4), side // 2], lax.rem(side, 2)


def device(q, core):
    return (q[0] * 4 + q[1], q[2] * 2 + core)


def peer(q, core, axis, k):
    to = list(q)
    to[axis] = lax.rem(q[axis] + k, 4)
    return device(to, core)


def split(v):
    hi = v.astype(BF16)
    return hi, (v - hi.astype(F32)).astype(BF16)


def dot(a, b, dims):
    return lax.dot_general(a, b, (dims, ((), ())), preferred_element_type=F32)


NN, TN, NT = ((1,), (0,)), ((0,), (0,)), ((1,), (1,))


def dot3(ah, al, bh, bl, dims):
    return dot(ah, bh, dims) + (dot(ah, bl, dims) + dot(al, bh, dims))


class Sum:
    def __init__(self, half, streams, x, out, halves, a, y, b, c, sems):
        self.half, self.streams, self.x, self.out = half, streams, x, out
        self.halves, self.a, self.y, self.b, self.c = halves, a, y, b, c
        self.send, self.recv = sems
        self.q, self.core = position()
        self.mine = self.core * half
        self.pending = []

    def copy(self, src, dst, slot, to):
        return pltpu.make_async_remote_copy(
            src_ref=src, dst_ref=dst, send_sem=self.send.at[slot], recv_sem=self.recv.at[slot],
            device_id=to, device_id_type=MESH)

    def start(self, src, dst, slot, to):
        copy = self.copy(src, dst, slot, to)
        copy.start()
        self.pending.append(copy)

    def arrive(self, ref, slot):
        self.copy(ref, ref, slot, device(self.q, 1 - self.core)).wait_recv()

    def rows(self, at, n):
        return pl.ds(pl.multiple_of(at, 8), n)

    def give(self, chunk, off, n):
        src = self.x.at[self.rows((1 - self.core) * self.half + off, n)]
        self.start(src, self.halves.at[pl.ds(off, n)], chunk, device(self.q, 1 - self.core))

    def take(self, chunk, off, n):
        self.arrive(self.halves.at[pl.ds(off, n)], chunk)
        at = self.rows(self.mine + off, n)
        self.x[at, :] += self.halves[pl.ds(off, n), :]

    def slot(self, phase, s, k):
        return 4 + phase * 9 + s * 3 + k - 1

    def phase_a(self, s):
        off, n = self.streams[s]
        axis = AXES[s][0]
        for k in (2, 1, 3):
            part = lax.rem(self.q[axis] + k, 4)
            src = self.x.at[self.rows(self.mine + off + part * (n // 4), n // 4)]
            dst = self.a.at[k - 1, pl.ds(off // 4, n // 4)]
            self.start(src, dst, self.slot(0, s, k), peer(self.q, self.core, axis, k))

    def phase_b(self, s):
        off, n = self.streams[s]
        axis, nxt = AXES[s][0], AXES[s][1]
        at = pl.ds(off // 4, n // 4)
        for k in (1, 3, 2):
            self.arrive(self.a.at[k - 1, at], self.slot(0, s, k))
        own = self.x[self.rows(self.mine + off + self.q[axis] * (n // 4), n // 4), :]
        self.y[at, :] = (own + self.a[0, at, :]) + (self.a[1, at, :] + self.a[2, at, :])
        for k in (2, 1, 3):
            part = lax.rem(self.q[nxt] + k, 4)
            src = self.y.at[at, pl.ds(pl.multiple_of(part * 128, 128), 128)]
            self.start(src, self.b.at[k - 1, at], self.slot(1, s, k), peer(self.q, self.core, nxt, k))

    def phase_c(self, s):
        off, n = self.streams[s]
        axis, nxt = AXES[s][1], AXES[s][2]
        at = pl.ds(off // 4, n // 4)
        for k in (1, 3, 2):
            self.arrive(self.b.at[k - 1, at], self.slot(1, s, k))
        own = self.y[at, pl.ds(pl.multiple_of(self.q[axis] * 128, 128), 128)]
        me = self.q[nxt]
        self.c[me, at, :] = (own + self.b[0, at, :]) + (self.b[1, at, :] + self.b[2, at, :])
        for k in (2, 1, 3):
            self.start(self.c.at[me, at], self.c.at[me, at], self.slot(2, s, k), peer(self.q, self.core, nxt, k))

    def quarter(self, s, part):
        off, n = self.streams[s]
        return self.rows(self.mine + off + part * (n // 4), n // 4)

    def phase_d(self, s):
        off, n = self.streams[s]
        second, third = AXES[s][1], AXES[s][2]
        at = pl.ds(off // 4, n // 4)
        for k in (1, 3, 2):
            self.arrive(self.c.at[lax.rem(self.q[third] + 4 - k, 4), at], self.slot(2, s, k))
        rows = self.quarter(s, self.q[AXES[s][0]])
        columns = pl.ds(pl.multiple_of(self.q[second] * 128, 128), 128)
        self.out[rows, columns] = (self.c[0, at, :] + self.c[1, at, :]) + (self.c[2, at, :] + self.c[3, at, :])
        for k in (2, 1, 3):
            block = self.out.at[rows, columns]
            self.start(block, block, self.slot(3, s, k), peer(self.q, self.core, second, k))

    def phase_e(self, s):
        first, second = AXES[s][0], AXES[s][1]
        rows = self.quarter(s, self.q[first])
        for k in (1, 3, 2):
            part = lax.rem(self.q[second] + 4 - k, 4)
            columns = pl.ds(pl.multiple_of(part * 128, 128), 128)
            self.arrive(self.out.at[rows, columns], self.slot(3, s, k))
        for k in (2, 1, 3):
            self.start(self.out.at[rows], self.out.at[rows], self.slot(4, s, k), peer(self.q, self.core, first, k))
        self.start(self.out.at[rows], self.out.at[rows], 49 + s * 4, device(self.q, 1 - self.core))

    def phase_f(self, s, ks):
        first = AXES[s][0]
        for k in ks:
            rows = self.quarter(s, lax.rem(self.q[first] + 4 - k, 4))
            self.arrive(self.out.at[rows], self.slot(4, s, k))
            self.start(self.out.at[rows], self.out.at[rows], 49 + s * 4 + k, device(self.q, 1 - self.core))

    def finish(self):
        for s, (off, n) in enumerate(self.streams):
            for k in range(4):
                part = lax.rem(self.q[AXES[s][0]] + 4 - k, 4)
                rows = self.rows((1 - self.core) * self.half + off + part * (n // 4), n // 4)
                self.arrive(self.out.at[rows], 49 + s * 4 + k)
        for copy in self.pending:
            copy.wait_send()

    def torus(self):
        for phase in (self.phase_b, self.phase_c, self.phase_d, self.phase_e):
            for s in range(3):
                phase(s)
        for ks in ((1, 3), (2,)):
            for s in range(3):
                self.phase_f(s, ks)
        self.finish()


SEMS = 61
WIDE = ((0, 192), (192, 160), (352, 160))
SMALL = ((0, 64), (64, 64), (128, 64))


def project_kernel(scale, block, basis, ph, pl_, gram, coeffs, sh, sl, kh, kl, x1, h1, a1, y1, b1, c1,
                   x2, h2, a2, y2, b2, c2, send1, recv1, send2, recv2):
    q, core = position()
    barrier = pltpu.get_barrier_semaphore()
    partners = [device(q, 1 - core)] + [peer(q, core, axis, k) for axis in range(3) for k in (1, 2, 3)]
    for to in partners:
        pl.semaphore_signal(barrier, inc=1, device_id=to, device_id_type=MESH)

    @pl.loop(0, 8)
    def _(i):
        at = pl.ds(pl.multiple_of(i * 128, 128), 128)
        hi, lo = split(basis[at, :])
        sh[at, :] = hi
        sl[at, :] = lo
        hi, lo = split(block[at, :])
        kh[at, :] = hi
        kl[at, :] = lo

    def terms(at):
        columns = pl.ds(pl.multiple_of(at, 256), 256)
        x1[columns, :] = dot3(sh[:, columns], sl[:, columns], kh[...], kl[...], TN)

    first = Sum(512, WIDE, x1, coeffs, h1, a1, y1, b1, c1, (send1, recv1))
    for chunk in range(2):
        terms((1 - core) * 512 + chunk * 256)
        if chunk == 0:
            pl.semaphore_wait(barrier, len(partners))
        first.give(chunk, chunk * 256, 256)
    for chunk in range(2):
        terms(core * 512 + chunk * 256)
    first.take(0, 0, 256)
    first.phase_a(0)
    first.take(1, 256, 256)
    first.phase_a(1)
    first.phase_a(2)
    first.torus()

    @pl.loop(0, 4)
    def _(i):
        at = pl.ds(pl.multiple_of(i * 256, 256), 256)
        hi, lo = split(coeffs[at, :])
        kh[at, :] = hi
        kl[at, :] = lo

    @pl.loop(0, 4)
    def _(i):
        at = pl.ds(pl.multiple_of(i * 256, 256), 256)
        hi, lo = split(block[at, :] - dot3(sh[at, :], sl[at, :], kh[...], kl[...], NN))
        ph[at, :] = hi
        pl_[at, :] = lo

    left = pl.ds(0, 256)
    right = pl.ds(256, 256)
    x2[0:256, :] = dot3(ph[:, left], pl_[:, left], ph[...], pl_[...], TN) * scale
    corner = dot3(ph[:, right], pl_[:, right], ph[:, right], pl_[:, right], TN) * scale
    x2[256:384, 0:256] = corner[0:128]
    x2[256:384, 256:512] = corner[128:256]
    second = Sum(192, SMALL, x2, gram, h2, a2, y2, b2, c2, (send2, recv2))
    second.give(0, 0, 192)
    second.take(0, 0, 192)
    for s in range(3):
        second.phase_a(s)
    second.torus()


def buffers(half):
    return [
        pltpu.VMEM((2 * half, 512), F32), pltpu.VMEM((half, 512), F32), pltpu.VMEM((3, half // 4, 512), F32),
        pltpu.VMEM((half // 4, 512), F32), pltpu.VMEM((3, half // 4, 128), F32), pltpu.VMEM((4, half // 4, 128), F32),
    ]


def project(block, basis, rows_total):
    vmem = pl.BlockSpec(memory_space=pltpu.VMEM)
    return pl.pallas_call(
        functools.partial(project_kernel, 1.0 / rows_total),
        out_shape=[
            jax.ShapeDtypeStruct((1024, 512), BF16), jax.ShapeDtypeStruct((1024, 512), BF16),
            jax.ShapeDtypeStruct((384, 512), F32), jax.ShapeDtypeStruct((1024, 512), F32),
        ],
        in_specs=[vmem] * 2,
        out_specs=[vmem] * 4,
        scratch_shapes=[pltpu.VMEM((1024, 1024), BF16)] * 2 + [pltpu.VMEM((1024, 512), BF16)] * 2
        + buffers(512) + buffers(192) + [pltpu.SemaphoreType.DMA((SEMS,))] * 4,
        compiler_params=pltpu.CompilerParams(
            collective_id=0, has_side_effects=True, vmem_limit_bytes=56 * 2**20),
    )(block, basis)


def eliminate(t):
    sub = lax.broadcasted_iota(jnp.int32, (8, 128), 0)
    lane = lax.broadcasted_iota(jnp.int32, (8, 128), 1)
    def row(v, j):
        return jnp.broadcast_to(v[j:j+1, :], (8, 128))
    def col(v, c):
        return jnp.broadcast_to(v[:, c:c+1], (8, 128))
    for p in range(16):
        lo = 8*p
        v0 = t[lo:lo+8, 0:128]
        v1 = t[lo:lo+8, 128:256]
        cs = [col(v0, lo+k) for k in range(8)]
        u0 = v0; u1 = v1
        dm = jnp.ones((8,128), F32); rm = dm
        for j in range(8):
            d = row(cs[j], j)
            r = 1.0/d
            m = jnp.where(sub == j, 0.0, cs[j]*r)
            w0 = row(v0, j); w1 = row(v1, j)
            u0 = jnp.where(sub == j, w0, u0)
            u1 = jnp.where(sub == j, w1, u1)
            dm = jnp.where(sub == j, d, dm)
            rm = jnp.where(sub == j, r, rm)
            for k in range(j+1, 8):
                cs[k] = cs[k] - m*row(cs[k], j)
            v0 = v0 - m*w0
            v1 = v1 - m*w1
        s = jnp.sqrt(dm)
        q = 1.0/s
        t[lo:lo+8, 0:128] = jnp.where(lane >= sub+lo, u0*q, 0.0)
        t[lo:lo+8, 128:256] = u1*q
        z0 = v0*rm; z1 = v1*rm
        zr = [(row(z0,k), row(z1,k)) for k in range(8)]
        for i in range(p+1, 16):
            a0 = t[8*i:8*i+8, 0:128]
            a1 = t[8*i:8*i+8, 128:256]
            ci = [col(a0, lo+k) for k in range(8)]
            s0=[ci[k]*zr[k][0] for k in range(8)]
            s1=[ci[k]*zr[k][1] for k in range(8)]
            while len(s0)>1:
                s0=[s0[2*x]+s0[2*x+1] for x in range(len(s0)//2)]
                s1=[s1[2*x]+s1[2*x+1] for x in range(len(s1)//2)]
            t[8*i:8*i+8, 0:128] = a0 - s0[0]
            t[8*i:8*i+8, 128:256] = a1 - s1[0]


def exact(a, b, dims):
    return lax.dot_general(a, b, (dims, ((), ())), precision=HI, preferred_element_type=F32)


def factor_kernel(g, ph, pl_, coeffs, ortho, r, coeffs_out, s, t, w, sem):
    keep = pltpu.make_async_copy(coeffs, coeffs_out, sem)
    keep.start()
    n = 512
    s[0:256, 0:n] = g[0:256, :]
    s[256:384, 256:n] = g[256:384, 0:256]
    s[384:512, 256:n] = g[256:384, 256:n]
    s[:, n:2 * n] = jnp.zeros((n, n), F32)
    eye = lax.broadcasted_iota(jnp.int32, (128, 128), 0) == lax.broadcasted_iota(jnp.int32, (128, 128), 1)
    eye = jnp.where(eye, 1.0, 0.0)
    for b in range(4):
        s[b * 128 : b * 128 + 128, n + b * 128 : n + b * 128 + 128] = eye
    r[...] = jnp.zeros((n, n), F32)
    w[...] = jnp.zeros((n, n), F32)

    def body(step, carry):
        for b in range(4):
            @pl.when(step == b)
            def _():
                t[:, 0:128] = s[b * 128 : b * 128 + 128, b * 128 : b * 128 + 128]
        t[:, 128:256] = eye
        eliminate(t)
        for b in range(4):
            @pl.when(step == b)
            def _():
                lo, hi = b * 128, b * 128 + 128
                li = t[:, 128:256]
                r[lo:hi, lo:hi] = t[:, 0:128]
                w[lo:hi, lo:hi] = li
                if b:
                    w[lo:hi, 0:lo] = exact(li, s[lo:hi, n : n + lo], NN)
                if b < 3:
                    right = exact(li, s[lo:hi, hi:n], NN)
                    r[lo:hi, hi:n] = right
                    for c in range(b + 1, 4):
                        at = slice(c * 128, c * 128 + 128)
                        rc = right[:, (c - b - 1) * 128 : (c - b) * 128]
                        s[at, c * 128 : n] -= exact(rc, right[:, (c - b - 1) * 128 :], TN)
                        s[at, n : n + hi] -= exact(rc, w[lo:hi, 0:hi], TN)
        return carry

    lax.fori_loop(0, 4, body, 0)
    for c in range(2):
        wh, wl = split(w[c * 256 : c * 256 + 256, 0 : c * 256 + 256])
        k = slice(0, c * 256 + 256)
        ortho[:, c * 256 : c * 256 + 256] = dot3(ph[:, k], pl_[:, k], wh, wl, NT)
    keep.wait()


def orthogonalize(gram, ph, pl_, coeffs):
    vmem = pl.BlockSpec(memory_space=pltpu.VMEM)
    anywhere = pl.BlockSpec(memory_space=pl.ANY)
    return pl.pallas_call(
        factor_kernel,
        out_shape=[
            jax.ShapeDtypeStruct((1024, 512), F32), jax.ShapeDtypeStruct((512, 512), F32),
            jax.ShapeDtypeStruct((1024, 512), F32),
        ],
        in_specs=[vmem] * 3 + [anywhere],
        out_specs=[vmem] * 2 + [anywhere],
        scratch_shapes=[
            pltpu.VMEM((512, 1024), F32), pltpu.VMEM((128, 256), F32), pltpu.VMEM((512, 512), F32),
            pltpu.SemaphoreType.DMA,
        ],
        compiler_params=pltpu.CompilerParams(vmem_limit_bytes=48 * 2**20),
    )(gram, ph, pl_, coeffs)


def shards(block, basis):
    rows_total = block.shape[0] * lax.axis_size("leaf") * lax.axis_size("side")
    ph, pl_, gram, coeffs = project(block, basis, rows_total)
    return orthogonalize(gram, ph, pl_, coeffs)


def solution(mesh):
    return jax.shard_map(
        shards,
        mesh=mesh,
        in_specs=(P(("leaf", "side"), None), P(("leaf", "side"), None)),
        out_specs=(P(("leaf", "side"), None), P(), P()),
        check_vma=False,
    )
```

```python
import functools
import jax
import jax.numpy as jnp
from jax import lax
from jax.experimental import pallas as pl
from jax.experimental.pallas import tpu as pltpu
from jax.sharding import PartitionSpec as P

F32 = jnp.float32
BF16 = jnp.bfloat16
MESH = pl.DeviceIdType.MESH
HI = lax.Precision.HIGHEST
AXES = ((0, 1, 2), (1, 2, 0), (2, 0, 1))


def position():
    leaf, side = lax.axis_index("leaf"), lax.axis_index("side")
    return [leaf // 4, lax.rem(leaf, 4), side // 2], lax.rem(side, 2)


def device(q, core):
    return (q[0] * 4 + q[1], q[2] * 2 + core)


def peer(q, core, axis, k, second=None, k2=0):
    to = list(q)
    to[axis] = lax.rem(q[axis] + k, 4)
    if second is not None:
        to[second] = lax.rem(q[second] + k2, 4)
    return device(to, core)


def split(v):
    hi = v.astype(BF16)
    return hi, (v - hi.astype(F32)).astype(BF16)


def dot(a, b, dims):
    return lax.dot_general(a, b, (dims, ((), ())), preferred_element_type=F32)


NN, TN, NT = ((1,), (0,)), ((0,), (0,)), ((1,), (1,))


def dot3(ah, al, bh, bl, dims):
    return dot(ah, bh, dims) + (dot(ah, bl, dims) + dot(al, bh, dims))


class Sum:
    def __init__(self, half, stride, base, streams, x, out, halves, a, y, b, c, send, recv):
        self.half, self.streams, self.x, self.out = half, streams, x, out
        self.halves, self.a, self.y, self.b, self.c = halves, a, y, b, c
        self.send, self.recv = send, recv
        self.q, self.core = position()
        self.mine = self.core * stride + base
        self.other = (1 - self.core) * stride + base
        self.pending = []

    def copy(self, src, dst, slot, to):
        return pltpu.make_async_remote_copy(
            src_ref=src, dst_ref=dst, send_sem=self.send.at[slot], recv_sem=self.recv.at[slot],
            device_id=to, device_id_type=MESH)

    def start(self, src, dst, slot, to):
        copy = self.copy(src, dst, slot, to)
        copy.start()
        self.pending.append(copy)

    def arrive(self, ref, slot):
        self.copy(ref, ref, slot, device(self.q, 1 - self.core)).wait_recv()

    def rows(self, at, n):
        return pl.ds(pl.multiple_of(at, 8), n)

    def give(self):
        chunk, off, n = 0, 0, self.half
        src = self.x.at[self.rows(self.other + off, n)]
        self.start(src, self.halves.at[pl.ds(off, n)], chunk, device(self.q, 1 - self.core))

    def take(self):
        chunk, off, n = 0, 0, self.half
        self.arrive(self.halves.at[pl.ds(off, n)], chunk)
        at = self.rows(self.mine + off, n)
        self.x[at, :] += self.halves[pl.ds(off, n), :]

    def slot(self, phase, s, k):
        return 4 + phase * 9 + s * 3 + k - 1

    def phase_a(self, s):
        off, n = self.streams[s]
        axis = AXES[s][0]
        for k in (2, 1, 3):
            part = lax.rem(self.q[axis] + k, 4)
            src = self.x.at[self.rows(self.mine + off + part * (n // 4), n // 4)]
            dst = self.a.at[k - 1, pl.ds(off // 4, n // 4)]
            self.start(src, dst, self.slot(0, s, k), peer(self.q, self.core, axis, k))

    def phase_b(self, s):
        off, n = self.streams[s]
        axis, nxt = AXES[s][0], AXES[s][1]
        at = pl.ds(off // 4, n // 4)
        for k in (1, 3, 2):
            self.arrive(self.a.at[k - 1, at], self.slot(0, s, k))
        own = self.x[self.rows(self.mine + off + self.q[axis] * (n // 4), n // 4), :]
        self.y[at, :] = (own + self.a[0, at, :]) + (self.a[1, at, :] + self.a[2, at, :])
        for k in (2, 1, 3):
            part = lax.rem(self.q[nxt] + k, 4)
            src = self.y.at[at, pl.ds(pl.multiple_of(part * 128, 128), 128)]
            self.start(src, self.b.at[k - 1, at], self.slot(1, s, k), peer(self.q, self.core, nxt, k))

    def phase_c(self, s):
        off, n = self.streams[s]
        axis, nxt = AXES[s][1], AXES[s][2]
        at = pl.ds(off // 4, n // 4)
        for k in (1, 3, 2):
            self.arrive(self.b.at[k - 1, at], self.slot(1, s, k))
        own = self.y[at, pl.ds(pl.multiple_of(self.q[axis] * 128, 128), 128)]
        me = self.q[nxt]
        self.c[me, at, :] = (own + self.b[0, at, :]) + (self.b[1, at, :] + self.b[2, at, :])
        for k in (2, 1, 3):
            self.start(self.c.at[me, at], self.c.at[me, at], self.slot(2, s, k), peer(self.q, self.core, nxt, k))

    def quarter(self, s, part):
        off, n = self.streams[s]
        return self.rows(self.mine + off + part * (n // 4), n // 4)

    def phase_d(self, s):
        off, n = self.streams[s]
        second, third = AXES[s][1], AXES[s][2]
        at = pl.ds(off // 4, n // 4)
        for k in (1, 3, 2):
            self.arrive(self.c.at[lax.rem(self.q[third] + 4 - k, 4), at], self.slot(2, s, k))
        rows = self.quarter(s, self.q[AXES[s][0]])
        columns = pl.ds(pl.multiple_of(self.q[second] * 128, 128), 128)
        self.out[rows, columns] = (self.c[0, at, :] + self.c[1, at, :]) + (self.c[2, at, :] + self.c[3, at, :])
        for k in (2, 1, 3):
            block = self.out.at[rows, columns]
            self.start(block, block, self.slot(3, s, k), peer(self.q, self.core, second, k))

    def phase_e(self, s):
        first, second = AXES[s][0], AXES[s][1]
        rows = self.quarter(s, self.q[first])
        for k in (1, 3, 2):
            part = lax.rem(self.q[second] + 4 - k, 4)
            columns = pl.ds(pl.multiple_of(part * 128, 128), 128)
            self.arrive(self.out.at[rows, columns], self.slot(3, s, k))
        for k in (2, 1, 3):
            self.start(self.out.at[rows], self.out.at[rows], self.slot(4, s, k), peer(self.q, self.core, first, k))
        self.start(self.out.at[rows], self.out.at[rows], 49 + s * 4, device(self.q, 1 - self.core))

    def phase_f(self, s, ks):
        first = AXES[s][0]
        for k in ks:
            rows = self.quarter(s, lax.rem(self.q[first] + 4 - k, 4))
            self.arrive(self.out.at[rows], self.slot(4, s, k))
            self.start(self.out.at[rows], self.out.at[rows], 49 + s * 4 + k, device(self.q, 1 - self.core))

    def meet(self):
        for s, (off, n) in enumerate(self.streams):
            for k in range(4):
                part = lax.rem(self.q[AXES[s][0]] + 4 - k, 4)
                self.arrive(self.out.at[self.rows(self.other + off + part * (n // 4), n // 4)], 49 + s * 4 + k)

    def drain(self):
        for copy in self.pending:
            copy.wait_send()


class PlaneSum(Sum):
    def plane(self, gather, s, k, k2):
        return 61 + gather * 45 + s * 15 + k * 4 + k2 - 1

    def scatter(self, s):
        off, n = self.streams[s]
        first, second = AXES[s][0], AXES[s][1]
        at = pl.ds(off // 4, n // 4)
        for k, k2 in STEPS:
            rows = self.quarter(s, lax.rem(self.q[first] + k, 4), self.x)
            columns = self.columns(lax.rem(self.q[second] + k2, 4))
            self.start(self.x.at[rows, columns], self.b.at[k * 4 + k2 - 1, at], self.plane(0, s, k, k2),
                       peer(self.q, self.core, first, k, second, k2))

    def columns(self, part):
        return pl.ds(pl.multiple_of(part * 128, 128), 128)

    def quarter(self, s, part, ref=None):
        off, n = self.streams[s]
        return self.rows(self.mine + off + part * (n // 4), n // 4)

    def exchange(self, s):
        off, n = self.streams[s]
        first, second, third = AXES[s]
        at = pl.ds(off // 4, n // 4)
        for k, k2 in STEPS[::-1]:
            self.arrive(self.b.at[k * 4 + k2 - 1, at], self.plane(0, s, k, k2))
        parts = [self.b[i, at, :] for i in range(15)]
        parts.append(self.x[self.quarter(s, self.q[first]), self.columns(self.q[second])])
        while len(parts) > 1:
            parts = [parts[i] + parts[i + 1] for i in range(0, len(parts), 2)]
        me = self.q[third]
        self.c[me, at, :] = parts[0]
        for k in (2, 1, 3):
            self.start(self.c.at[me, at], self.c.at[me, at], self.slot(2, s, k), peer(self.q, self.core, third, k))

    def gather(self, s):
        off, n = self.streams[s]
        first, second, third = AXES[s]
        at = pl.ds(off // 4, n // 4)
        for k in (1, 3, 2):
            self.arrive(self.c.at[lax.rem(self.q[third] + 4 - k, 4), at], self.slot(2, s, k))
        block = self.out.at[self.quarter(s, self.q[first]), self.columns(self.q[second])]
        block[...] = (self.c[0, at, :] + self.c[1, at, :]) + (self.c[2, at, :] + self.c[3, at, :])
        for k, k2 in STEPS:
            self.start(block, block, self.plane(1, s, k, k2), peer(self.q, self.core, first, k, second, k2))

    def forward(self, s, ks):
        first, second = AXES[s][0], AXES[s][1]
        for k in ks:
            rows = self.quarter(s, lax.rem(self.q[first] + 4 - k, 4))
            for k2 in (0, 1, 3, 2):
                if k or k2:
                    block = self.out.at[rows, self.columns(lax.rem(self.q[second] + 4 - k2, 4))]
                    self.arrive(block, self.plane(1, s, k, k2))
            self.start(self.out.at[rows], self.out.at[rows], 49 + s * 4 + k, device(self.q, 1 - self.core))


STEPS = tuple((k, k2) for k in (2, 1, 3, 0) for k2 in (2, 1, 3, 0) if k or k2)


WIDE = ((0, 96), (96, 96), (192, 64))
SMALL = ((0, 64), (64, 64), (128, 64))


def project_kernel(scale, block_in, basis_in, ph_out, pl_out, gram, coeffs_out, bs, bk, sh, sl, kh, kl, ph, pl_, x1, coeffs, x2,
                   load, *rest):
    buffers0, buffers1, buffers2, store = rest[0:7], rest[7:14], rest[14:20], rest[20]
    q, core = position()
    loads = []
    for i in range(4):
        at = pl.ds(i * 256, 256)
        loads.append((pltpu.make_async_copy(basis_in.at[at], bs.at[at], load.at[0, i]),
                      pltpu.make_async_copy(block_in.at[at], bk.at[at], load.at[1, i])))
    for pair in loads:
        for copy in pair:
            copy.start()
    barrier = pltpu.get_barrier_semaphore()
    partners = [device(q, 1 - core)] + [peer(q, core, axis, k) for axis in range(3) for k in (1, 2, 3)]
    partners += [peer(q, core, first, k, second, k2) for first, second, _ in AXES for k in (1, 2, 3) for k2 in (1, 2, 3)]
    for to in partners:
        pl.semaphore_signal(barrier, inc=1, device_id=to, device_id_type=MESH)

    for i in range(4):
        for copy in loads[i]:
            copy.wait()

        @pl.loop(i * 2, i * 2 + 2)
        def _(j):
            at = pl.ds(pl.multiple_of(j * 128, 128), 128)
            hi, lo = split(bs[at, :])
            sh[at, :] = hi
            sl[at, :] = lo
            hi, lo = split(bk[at, :])
            kh[at, :] = hi
            kl[at, :] = lo

    def terms(at):
        columns = pl.ds(pl.multiple_of(at, 256), 256)
        x1[columns, :] = dot3(sh[:, columns], sl[:, columns], kh[...], kl[...], TN)

    sums = [Sum(256, 512, 256 * i, WIDE, x1, coeffs, *half) for i, half in enumerate((buffers0[:7], buffers1[:7]))]
    for i in range(2):
        terms((1 - core) * 512 + i * 256)
        if i == 0:
            pl.semaphore_wait(barrier, len(partners))
        sums[i].give()
    for i in range(2):
        terms(core * 512 + i * 256)
        sums[i].take()
        for s in range(3):
            sums[i].phase_a(s)
    for phase in ("phase_b", "phase_c", "phase_d", "phase_e"):
        for each in sums:
            for s in range(3):
                getattr(each, phase)(s)

    def subtract(at):
        rows = pl.ds(pl.multiple_of(at, 256), 256)
        hi, lo = split(coeffs[rows, :])
        kh[rows, :] = hi
        kl[rows, :] = lo

        @pl.loop(0, 4)
        def _(i):
            at = pl.ds(pl.multiple_of(i * 256, 256), 256)
            bk[at, :] -= dot3(sh[at, rows], sl[at, rows], kh[rows, :], kl[rows, :], NN)

    for i in range(2):
        for ks in ((1, 3), (2,)):
            for s in range(3):
                sums[i].phase_f(s, ks)
        subtract(core * 512 + i * 256)
    for i in range(2):
        sums[i].meet()
        subtract((1 - core) * 512 + i * 256)

    keep = [pltpu.make_async_copy(coeffs, coeffs_out, store.at[0])]
    keep[0].start()

    @pl.loop(0, 4)
    def _(i):
        at = pl.ds(pl.multiple_of(i * 256, 256), 256)
        hi, lo = split(bk[at, :])
        ph[at, :] = hi
        pl_[at, :] = lo

    keep += [pltpu.make_async_copy(ph, ph_out, store.at[1]), pltpu.make_async_copy(pl_, pl_out, store.at[2])]
    keep[1].start()
    keep[2].start()
    left = pl.ds(0, 256)
    right = pl.ds(256, 256)
    x2[0:256, :] = dot3(ph[:, left], pl_[:, left], ph[...], pl_[...], TN) * scale
    corner = dot3(ph[:, right], pl_[:, right], ph[:, right], pl_[:, right], TN) * scale
    x2[256:384, 0:256] = corner[0:128]
    x2[256:384, 256:512] = corner[128:256]
    halves, b, c, send, recv = buffers2[0], buffers2[1], buffers2[2], buffers2[3], buffers2[4]
    last = PlaneSum(192, 192, 0, SMALL, x2, gram, halves, None, None, b, c, send, recv)
    last.give()
    last.take()
    for phase in (last.scatter, last.exchange, last.gather):
        for s in range(3):
            phase(s)
    for ks in ((0, 1, 3), (2,)):
        for s in range(3):
            last.forward(s, ks)
    last.meet()
    for each in (*sums, last):
        each.drain()
    for copy in keep:
        copy.wait()


def buffers(half):
    return [
        pltpu.VMEM((half, 512), F32), pltpu.VMEM((3, half // 4, 512), F32), pltpu.VMEM((half // 4, 512), F32),
        pltpu.VMEM((3, half // 4, 128), F32), pltpu.VMEM((4, half // 4, 128), F32),
        pltpu.SemaphoreType.DMA((61,)), pltpu.SemaphoreType.DMA((61,)),
    ]


def project(block, basis, rows_total):
    anywhere = pl.BlockSpec(memory_space=pl.ANY)
    return pl.pallas_call(
        functools.partial(project_kernel, 1.0 / rows_total),
        out_shape=[
            jax.ShapeDtypeStruct((1024, 512), BF16), jax.ShapeDtypeStruct((1024, 512), BF16),
            jax.ShapeDtypeStruct((384, 512), F32), jax.ShapeDtypeStruct((1024, 512), F32),
        ],
        in_specs=[anywhere] * 2,
        out_specs=[anywhere, anywhere, pl.BlockSpec(memory_space=pltpu.VMEM), anywhere],
        scratch_shapes=[
            pltpu.VMEM((1024, 1024), F32), pltpu.VMEM((1024, 512), F32),
            pltpu.VMEM((1024, 1024), BF16), pltpu.VMEM((1024, 1024), BF16),
            pltpu.VMEM((1024, 512), BF16), pltpu.VMEM((1024, 512), BF16),
            pltpu.VMEM((1024, 512), BF16), pltpu.VMEM((1024, 512), BF16),
            pltpu.VMEM((1024, 512), F32), pltpu.VMEM((1024, 512), F32), pltpu.VMEM((384, 512), F32),
            pltpu.SemaphoreType.DMA((2, 4)),
            *buffers(256), *buffers(256),
            pltpu.VMEM((192, 512), F32), pltpu.VMEM((15, 48, 128), F32), pltpu.VMEM((4, 48, 128), F32),
            pltpu.SemaphoreType.DMA((151,)), pltpu.SemaphoreType.DMA((151,)), pltpu.SemaphoreType.DMA((1,)),
            pltpu.SemaphoreType.DMA((3,)),
        ],
        compiler_params=pltpu.CompilerParams(
            collective_id=0, has_side_effects=True, vmem_limit_bytes=60 * 2**20),
    )(block, basis)


def eliminate(t):
    sub = lax.broadcasted_iota(jnp.int32, (8, 128), 0)
    lane = lax.broadcasted_iota(jnp.int32, (8, 128), 1)

    def row(v, j):
        return jnp.broadcast_to(v[j : j + 1, :], (8, 128))

    def col(v, c):
        return jnp.broadcast_to(v[:, c : c + 1], (8, 128))

    def update(i, lo, zr):
        a0 = t[8 * i : 8 * i + 8, 0:128]
        a1 = t[8 * i : 8 * i + 8, 128:256]
        ci = [col(a0, lo + k) for k in range(8)]
        s0 = [ci[k] * zr[k][0] for k in range(8)]
        s1 = [ci[k] * zr[k][1] for k in range(8)]
        while len(s0) > 1:
            s0 = [s0[x] + s0[x + 1] for x in range(0, len(s0), 2)]
            s1 = [s1[x] + s1[x + 1] for x in range(0, len(s1), 2)]
        v0, v1 = a0 - s0[0], a1 - s1[0]
        t[8 * i : 8 * i + 8, 0:128] = v0
        t[8 * i : 8 * i + 8, 128:256] = v1
        return v0, v1

    v0, v1 = t[0:8, 0:128], t[0:8, 128:256]
    for p in range(16):
        lo = 8 * p
        x = [col(v0, lo + k) for k in range(8)] + [v0, v1]
        raw0, raw1 = v0, v1
        a_of = jnp.ones((8, 128), F32)
        b_of = jnp.zeros((8, 128), F32)
        d_of = b_of
        for j in range(0, 8, 2):
            even, odd = sub == j, sub == j + 1
            pair = even | odd
            top = [row(v, j) if n > j else None for n, v in enumerate(x)]
            low = [row(v, j + 1) if n > j else None for n, v in enumerate(x)]
            a, b, c = row(x[j], j), top[j + 1], low[j + 1]
            g = 1.0 / (a * c - b * b)
            n0 = jnp.where(even, c, jnp.where(odd, -b, x[j + 1] * b - x[j] * c))
            n1 = jnp.where(even, -b, jnp.where(odd, a, x[j] * b - x[j + 1] * a))
            raw0 = jnp.where(even, top[8], jnp.where(odd, low[8], raw0))
            raw1 = jnp.where(even, top[9], jnp.where(odd, low[9], raw1))
            a_of = jnp.where(odd, a, a_of)
            b_of = jnp.where(odd, b, b_of)
            d_of = jnp.where(even, a, jnp.where(odd, c, d_of))
            for n in range(j + 2, 10):
                x[n] = jnp.where(pair, 0.0, x[n]) + g * (n0 * top[n] + n1 * low[n])
        zr = [(row(x[8], k), row(x[9], k)) for k in range(8)]
        if p < 15:
            v0, v1 = update(p + 1, lo, zr)
        m = b_of / a_of
        q = 1.0 / jnp.sqrt(d_of - m * b_of)
        u0 = raw0 - m * pltpu.roll(raw0, 1, 0)
        u1 = raw1 - m * pltpu.roll(raw1, 1, 0)
        t[lo : lo + 8, 0:128] = jnp.where(lane >= sub + lo, u0 * q, 0.0)
        t[lo : lo + 8, 128:256] = u1 * q
        for i in range(p + 2, 16):
            update(i, lo, zr)


def exact(a, b, dims):
    return lax.dot_general(a, b, (dims, ((), ())), precision=HI, preferred_element_type=F32)


def factor_kernel(g_in, ph_in, pl_in, coeffs, ortho_out, r_out, coeffs_out, g, ph, pl_, ortho, r, s, t, w, root, sems):
    copies = [pltpu.make_async_copy(a, b, sems.at[i]) for i, (a, b) in enumerate(
        ((g_in, g), (ph_in, ph), (pl_in, pl_), (coeffs, coeffs_out)))]
    for copy in copies:
        copy.start()
    n = 512
    r[...] = jnp.zeros((n, n), F32)
    w[...] = jnp.zeros((n, n), F32)
    s[:, n : 2 * n] = jnp.zeros((n, n), F32)
    eye = lax.broadcasted_iota(jnp.int32, (128, 128), 0) == lax.broadcasted_iota(jnp.int32, (128, 128), 1)
    copies[0].wait()
    s[0:256, 0:n] = g[0:256, :]
    s[256:384, 256:n] = g[256:384, 0:256]
    s[384:512, 256:n] = g[256:384, 256:n]
    down = []
    for b in range(4):
        at = slice(b * 128, b * 128 + 128)
        diagonal = jnp.where(eye, s[at, at], 0.0)
        across = jnp.sqrt(jnp.sum(diagonal, axis=0, keepdims=True))
        root[0:1, at] = across
        root[1:2, at] = 1.0 / across
        s[at, n + b * 128 : n + b * 128 + 128] = jnp.where(eye, 1.0 / across, 0.0)
        down.append(1.0 / jnp.sqrt(jnp.sum(diagonal, axis=1, keepdims=True)))
    for b in range(4):
        at = slice(b * 128, b * 128 + 128)
        s[at, b * 128 : n] = s[at, b * 128 : n] * down[b] * root[1:2, b * 128 : n]

    def body(step, carry):
        for b in range(4):
            @pl.when(step == b)
            def _():
                t[:, 0:128] = s[b * 128 : b * 128 + 128, b * 128 : b * 128 + 128]
                t[:, 128:256] = s[b * 128 : b * 128 + 128, n + b * 128 : n + b * 128 + 128]
        eliminate(t)
        for b in range(4):
            @pl.when(step == b)
            def _():
                lo, hi = b * 128, b * 128 + 128
                scaled = t[:, 128:256]
                li = scaled * root[0:1, lo:hi]
                r[lo:hi, lo:hi] = t[:, 0:128] * root[0:1, lo:hi]
                w[lo:hi, lo:hi] = scaled
                if b:
                    w[lo:hi, 0:lo] = exact(li, s[lo:hi, n : n + lo], NN)
                if b < 3:
                    right = exact(li, s[lo:hi, hi:n], NN)
                    r[lo:hi, hi:n] = right * root[0:1, hi:n]
                    for c in range(b + 1, 4):
                        at = slice(c * 128, c * 128 + 128)
                        rc = right[:, (c - b - 1) * 128 : (c - b) * 128]
                        s[at, c * 128 : n] -= exact(rc, right[:, (c - b - 1) * 128 :], TN)
                        s[at, n : n + hi] -= exact(rc, w[lo:hi, 0:hi], TN)
        return carry

    lax.fori_loop(0, 4, body, 0)
    stores = [pltpu.make_async_copy(r, r_out, sems.at[4])]
    stores[0].start()
    copies[1].wait()
    copies[2].wait()
    wh, wl = split(w[...])
    for i in range(4):
        rows = slice(i * 256, i * 256 + 256)
        for c in range(2):
            at, k = slice(c * 256, c * 256 + 256), slice(0, c * 256 + 256)
            ortho[rows, at] = dot3(ph[rows, k], pl_[rows, k], wh[at, k], wl[at, k], NT)
        stores.append(pltpu.make_async_copy(ortho.at[pl.ds(i * 256, 256)], ortho_out.at[pl.ds(i * 256, 256)], sems.at[5 + i]))
        stores[-1].start()
    copies[3].wait()
    for copy in stores:
        copy.wait()


def orthogonalize(gram, ph, pl_, coeffs):
    anywhere = pl.BlockSpec(memory_space=pl.ANY)
    return pl.pallas_call(
        factor_kernel,
        out_shape=[
            jax.ShapeDtypeStruct((1024, 512), F32), jax.ShapeDtypeStruct((512, 512), F32),
            jax.ShapeDtypeStruct((1024, 512), F32),
        ],
        in_specs=[anywhere] * 4,
        out_specs=[anywhere] * 3,
        scratch_shapes=[
            pltpu.VMEM((384, 512), F32), pltpu.VMEM((1024, 512), BF16), pltpu.VMEM((1024, 512), BF16),
            pltpu.VMEM((1024, 512), F32), pltpu.VMEM((512, 512), F32),
            pltpu.VMEM((512, 1024), F32), pltpu.VMEM((128, 256), F32), pltpu.VMEM((512, 512), F32),
            pltpu.VMEM((8, 512), F32), pltpu.SemaphoreType.DMA((9,)),
        ],
        compiler_params=pltpu.CompilerParams(vmem_limit_bytes=63 * 2**20),
    )(gram, ph, pl_, coeffs)


def shards(block, basis):
    rows_total = block.shape[0] * lax.axis_size("leaf") * lax.axis_size("side")
    ph, pl_, gram, coeffs = project(block, basis, rows_total)
    return orthogonalize(gram, ph, pl_, coeffs)


def solution(mesh):
    return jax.shard_map(
        shards,
        mesh=mesh,
        in_specs=(P(("leaf", "side"), None), P(("leaf", "side"), None)),
        out_specs=(P(("leaf", "side"), None), P(), P()),
        check_vma=False,
    )
```

```python
import functools
import jax
import jax.numpy as jnp
from jax import lax
from jax.experimental import pallas as pl
from jax.experimental.pallas import tpu as pltpu
from jax.sharding import PartitionSpec as P

F32 = jnp.float32
BF16 = jnp.bfloat16
MESH = pl.DeviceIdType.MESH
HI = lax.Precision.HIGHEST
AXES = ((0, 1, 2), (1, 2, 0), (2, 0, 1))


def position():
    leaf, side = lax.axis_index("leaf"), lax.axis_index("side")
    return [leaf // 4, lax.rem(leaf, 4), side // 2], lax.rem(side, 2)


def device(q, core):
    return (q[0] * 4 + q[1], q[2] * 2 + core)


def peer(q, core, axis, k, second=None, k2=0):
    to = list(q)
    to[axis] = lax.rem(q[axis] + k, 4)
    if second is not None:
        to[second] = lax.rem(q[second] + k2, 4)
    return device(to, core)


def split(v):
    hi = v.astype(BF16)
    return hi, (v - hi.astype(F32)).astype(BF16)


def dot(a, b, dims):
    return lax.dot_general(a, b, (dims, ((), ())), preferred_element_type=F32)


NN, TN, NT = ((1,), (0,)), ((0,), (0,)), ((1,), (1,))


def dot3(ah, al, bh, bl, dims):
    return dot(ah, bh, dims) + (dot(ah, bl, dims) + dot(al, bh, dims))


class Sum:
    def __init__(self, half, stride, base, streams, x, out, halves, a, y, b, c, send, recv):
        self.half, self.streams, self.x, self.out = half, streams, x, out
        self.halves, self.a, self.y, self.b, self.c = halves, a, y, b, c
        self.send, self.recv = send, recv
        self.q, self.core = position()
        self.mine = self.core * stride + base
        self.other = (1 - self.core) * stride + base
        self.pending = []

    def copy(self, src, dst, slot, to):
        return pltpu.make_async_remote_copy(
            src_ref=src, dst_ref=dst, send_sem=self.send.at[slot], recv_sem=self.recv.at[slot],
            device_id=to, device_id_type=MESH)

    def start(self, src, dst, slot, to):
        copy = self.copy(src, dst, slot, to)
        copy.start()
        self.pending.append(copy)

    def arrive(self, ref, slot):
        self.copy(ref, ref, slot, device(self.q, 1 - self.core)).wait_recv()

    def rows(self, at, n):
        return pl.ds(pl.multiple_of(at, 8), n)

    def give(self):
        chunk, off, n = 0, 0, self.half
        src = self.x.at[self.rows(self.other + off, n)]
        self.start(src, self.halves.at[pl.ds(off, n)], chunk, device(self.q, 1 - self.core))

    def take(self):
        chunk, off, n = 0, 0, self.half
        self.arrive(self.halves.at[pl.ds(off, n)], chunk)
        at = self.rows(self.mine + off, n)
        self.x[at, :] += self.halves[pl.ds(off, n), :]

    def slot(self, phase, s, k):
        return 4 + phase * 9 + s * 3 + k - 1

    def phase_a(self, s):
        off, n = self.streams[s]
        axis = AXES[s][0]
        for k in (2, 1, 3):
            part = lax.rem(self.q[axis] + k, 4)
            src = self.x.at[self.rows(self.mine + off + part * (n // 4), n // 4)]
            dst = self.a.at[k - 1, pl.ds(off // 4, n // 4)]
            self.start(src, dst, self.slot(0, s, k), peer(self.q, self.core, axis, k))

    def phase_b(self, s):
        off, n = self.streams[s]
        axis, nxt = AXES[s][0], AXES[s][1]
        at = pl.ds(off // 4, n // 4)
        for k in (1, 3, 2):
            self.arrive(self.a.at[k - 1, at], self.slot(0, s, k))
        own = self.x[self.rows(self.mine + off + self.q[axis] * (n // 4), n // 4), :]
        self.y[at, :] = (own + self.a[0, at, :]) + (self.a[1, at, :] + self.a[2, at, :])
        for k in (2, 1, 3):
            part = lax.rem(self.q[nxt] + k, 4)
            src = self.y.at[at, pl.ds(pl.multiple_of(part * 128, 128), 128)]
            self.start(src, self.b.at[k - 1, at], self.slot(1, s, k), peer(self.q, self.core, nxt, k))

    def phase_c(self, s):
        off, n = self.streams[s]
        axis, nxt = AXES[s][1], AXES[s][2]
        at = pl.ds(off // 4, n // 4)
        for k in (1, 3, 2):
            self.arrive(self.b.at[k - 1, at], self.slot(1, s, k))
        own = self.y[at, pl.ds(pl.multiple_of(self.q[axis] * 128, 128), 128)]
        me = self.q[nxt]
        self.c[me, at, :] = (own + self.b[0, at, :]) + (self.b[1, at, :] + self.b[2, at, :])
        for k in (2, 1, 3):
            self.start(self.c.at[me, at], self.c.at[me, at], self.slot(2, s, k), peer(self.q, self.core, nxt, k))

    def quarter(self, s, part):
        off, n = self.streams[s]
        return self.rows(self.mine + off + part * (n // 4), n // 4)

    def phase_d(self, s):
        off, n = self.streams[s]
        second, third = AXES[s][1], AXES[s][2]
        at = pl.ds(off // 4, n // 4)
        for k in (1, 3, 2):
            self.arrive(self.c.at[lax.rem(self.q[third] + 4 - k, 4), at], self.slot(2, s, k))
        rows = self.quarter(s, self.q[AXES[s][0]])
        columns = pl.ds(pl.multiple_of(self.q[second] * 128, 128), 128)
        self.out[rows, columns] = (self.c[0, at, :] + self.c[1, at, :]) + (self.c[2, at, :] + self.c[3, at, :])
        for k in (2, 1, 3):
            block = self.out.at[rows, columns]
            self.start(block, block, self.slot(3, s, k), peer(self.q, self.core, second, k))

    def phase_e(self, s):
        first, second = AXES[s][0], AXES[s][1]
        rows = self.quarter(s, self.q[first])
        for k in (1, 3, 2):
            part = lax.rem(self.q[second] + 4 - k, 4)
            columns = pl.ds(pl.multiple_of(part * 128, 128), 128)
            self.arrive(self.out.at[rows, columns], self.slot(3, s, k))
        for k in (2, 1, 3):
            self.start(self.out.at[rows], self.out.at[rows], self.slot(4, s, k), peer(self.q, self.core, first, k))
        self.start(self.out.at[rows], self.out.at[rows], 49 + s * 4, device(self.q, 1 - self.core))

    def phase_f(self, s, ks):
        first = AXES[s][0]
        for k in ks:
            rows = self.quarter(s, lax.rem(self.q[first] + 4 - k, 4))
            self.arrive(self.out.at[rows], self.slot(4, s, k))
            self.start(self.out.at[rows], self.out.at[rows], 49 + s * 4 + k, device(self.q, 1 - self.core))

    def meet(self):
        for s, (off, n) in enumerate(self.streams):
            for k in range(4):
                part = lax.rem(self.q[AXES[s][0]] + 4 - k, 4)
                self.arrive(self.out.at[self.rows(self.other + off + part * (n // 4), n // 4)], 49 + s * 4 + k)

    def drain(self):
        for copy in self.pending:
            copy.wait_send()


class PlaneSum(Sum):
    def plane(self, gather, s, k, k2):
        return 61 + gather * 45 + s * 15 + k * 4 + k2 - 1

    def scatter(self, s):
        off, n = self.streams[s]
        first, second = AXES[s][0], AXES[s][1]
        at = pl.ds(off // 4, n // 4)
        for k, k2 in STEPS:
            rows = self.quarter(s, lax.rem(self.q[first] + k, 4), self.x)
            columns = self.columns(lax.rem(self.q[second] + k2, 4))
            self.start(self.x.at[rows, columns], self.b.at[k * 4 + k2 - 1, at], self.plane(0, s, k, k2),
                       peer(self.q, self.core, first, k, second, k2))

    def columns(self, part):
        return pl.ds(pl.multiple_of(part * 128, 128), 128)

    def quarter(self, s, part, ref=None):
        off, n = self.streams[s]
        return self.rows(self.mine + off + part * (n // 4), n // 4)

    def exchange(self, s):
        off, n = self.streams[s]
        first, second, third = AXES[s]
        at = pl.ds(off // 4, n // 4)
        for k, k2 in STEPS[::-1]:
            self.arrive(self.b.at[k * 4 + k2 - 1, at], self.plane(0, s, k, k2))
        parts = [self.b[i, at, :] for i in range(15)]
        parts.append(self.x[self.quarter(s, self.q[first]), self.columns(self.q[second])])
        while len(parts) > 1:
            parts = [parts[i] + parts[i + 1] for i in range(0, len(parts), 2)]
        me = self.q[third]
        self.c[me, at, :] = parts[0]
        for k in (2, 1, 3):
            self.start(self.c.at[me, at], self.c.at[me, at], self.slot(2, s, k), peer(self.q, self.core, third, k))

    def gather(self, s):
        off, n = self.streams[s]
        first, second, third = AXES[s]
        at = pl.ds(off // 4, n // 4)
        for k in (1, 3, 2):
            self.arrive(self.c.at[lax.rem(self.q[third] + 4 - k, 4), at], self.slot(2, s, k))
        block = self.out.at[self.quarter(s, self.q[first]), self.columns(self.q[second])]
        block[...] = (self.c[0, at, :] + self.c[1, at, :]) + (self.c[2, at, :] + self.c[3, at, :])
        for k, k2 in STEPS:
            self.start(block, block, self.plane(1, s, k, k2), peer(self.q, self.core, first, k, second, k2))

    def forward(self, s, ks):
        first, second = AXES[s][0], AXES[s][1]
        for k in ks:
            rows = self.quarter(s, lax.rem(self.q[first] + 4 - k, 4))
            for k2 in (0, 1, 3, 2):
                if k or k2:
                    block = self.out.at[rows, self.columns(lax.rem(self.q[second] + 4 - k2, 4))]
                    self.arrive(block, self.plane(1, s, k, k2))
            self.start(self.out.at[rows], self.out.at[rows], 49 + s * 4 + k, device(self.q, 1 - self.core))


STEPS = tuple((k, k2) for k in (2, 1, 3, 0) for k2 in (2, 1, 3, 0) if k or k2)


WIDE = ((0, 96), (96, 96), (192, 64))
SMALL = ((0, 64), (64, 64), (128, 64))


def project_kernel(scale, block_in, basis_in, ph_out, pl_out, gram, coeffs_out, bs, bk, sh, sl, kh, kl, ph, pl_, x1, coeffs, x2,
                   load, *rest):
    buffers0, buffers1, buffers2, store = rest[0:7], rest[7:14], rest[14:20], rest[20]
    q, core = position()
    loads = []
    for i in range(4):
        at = pl.ds(i * 256, 256)
        loads.append((pltpu.make_async_copy(basis_in.at[at], bs.at[at], load.at[0, i]),
                      pltpu.make_async_copy(block_in.at[at], bk.at[at], load.at[1, i])))
    for pair in loads:
        for copy in pair:
            copy.start()
    barrier = pltpu.get_barrier_semaphore()
    partners = [device(q, 1 - core)] + [peer(q, core, axis, k) for axis in range(3) for k in (1, 2, 3)]
    partners += [peer(q, core, first, k, second, k2) for first, second, _ in AXES for k in (1, 2, 3) for k2 in (1, 2, 3)]
    for to in partners:
        pl.semaphore_signal(barrier, inc=1, device_id=to, device_id_type=MESH)

    for i in range(4):
        for copy in loads[i]:
            copy.wait()

        @pl.loop(i * 2, i * 2 + 2)
        def _(j):
            at = pl.ds(pl.multiple_of(j * 128, 128), 128)
            hi, lo = split(bs[at, :])
            sh[at, :] = hi
            sl[at, :] = lo
            hi, lo = split(bk[at, :])
            kh[at, :] = hi
            kl[at, :] = lo

    def terms(at):
        columns = pl.ds(pl.multiple_of(at, 256), 256)
        x1[columns, :] = dot3(sh[:, columns], sl[:, columns], kh[...], kl[...], TN)

    sums = [Sum(256, 512, 256 * i, WIDE, x1, coeffs, *half) for i, half in enumerate((buffers0[:7], buffers1[:7]))]
    for i in range(2):
        terms((1 - core) * 512 + i * 256)
        if i == 0:
            pl.semaphore_wait(barrier, len(partners))
        sums[i].give()
    for i in range(2):
        terms(core * 512 + i * 256)
        sums[i].take()
        for s in range(3):
            sums[i].phase_a(s)
    for phase in ("phase_b", "phase_c", "phase_d", "phase_e"):
        for each in sums:
            for s in range(3):
                getattr(each, phase)(s)

    def subtract(at):
        rows = pl.ds(pl.multiple_of(at, 256), 256)
        hi, lo = split(coeffs[rows, :])
        kh[rows, :] = hi
        kl[rows, :] = lo

        @pl.loop(0, 4)
        def _(i):
            at = pl.ds(pl.multiple_of(i * 256, 256), 256)
            bk[at, :] -= dot3(sh[at, rows], sl[at, rows], kh[rows, :], kl[rows, :], NN)

    for i in range(2):
        for ks in ((1, 3), (2,)):
            for s in range(3):
                sums[i].phase_f(s, ks)
        subtract(core * 512 + i * 256)
    for i in range(2):
        sums[i].meet()
        subtract((1 - core) * 512 + i * 256)

    keep = [pltpu.make_async_copy(coeffs, coeffs_out, store.at[0])]
    keep[0].start()

    @pl.loop(0, 4)
    def _(i):
        at = pl.ds(pl.multiple_of(i * 256, 256), 256)
        hi, lo = split(bk[at, :])
        ph[at, :] = hi
        pl_[at, :] = lo

    keep += [pltpu.make_async_copy(ph, ph_out, store.at[1]), pltpu.make_async_copy(pl_, pl_out, store.at[2])]
    keep[1].start()
    keep[2].start()
    left = pl.ds(0, 256)
    right = pl.ds(256, 256)
    x2[0:256, :] = dot3(ph[:, left], pl_[:, left], ph[...], pl_[...], TN) * scale
    corner = dot3(ph[:, right], pl_[:, right], ph[:, right], pl_[:, right], TN) * scale
    x2[256:384, 0:256] = corner[0:128]
    x2[256:384, 256:512] = corner[128:256]
    halves, b, c, send, recv = buffers2[0], buffers2[1], buffers2[2], buffers2[3], buffers2[4]
    last = PlaneSum(192, 192, 0, SMALL, x2, gram, halves, None, None, b, c, send, recv)
    last.give()
    last.take()
    for phase in (last.scatter, last.exchange, last.gather):
        for s in range(3):
            phase(s)
    for ks in ((0, 1, 3), (2,)):
        for s in range(3):
            last.forward(s, ks)
    last.meet()
    for each in (*sums, last):
        each.drain()
    for copy in keep:
        copy.wait()


def buffers(half):
    return [
        pltpu.VMEM((half, 512), F32), pltpu.VMEM((3, half // 4, 512), F32), pltpu.VMEM((half // 4, 512), F32),
        pltpu.VMEM((3, half // 4, 128), F32), pltpu.VMEM((4, half // 4, 128), F32),
        pltpu.SemaphoreType.DMA((61,)), pltpu.SemaphoreType.DMA((61,)),
    ]


def project(block, basis, rows_total):
    anywhere = pl.BlockSpec(memory_space=pl.ANY)
    return pl.pallas_call(
        functools.partial(project_kernel, 1.0 / rows_total),
        out_shape=[
            jax.ShapeDtypeStruct((1024, 512), BF16), jax.ShapeDtypeStruct((1024, 512), BF16),
            jax.ShapeDtypeStruct((384, 512), F32), jax.ShapeDtypeStruct((1024, 512), F32),
        ],
        in_specs=[anywhere] * 2,
        out_specs=[anywhere, anywhere, pl.BlockSpec(memory_space=pltpu.VMEM), anywhere],
        scratch_shapes=[
            pltpu.VMEM((1024, 1024), F32), pltpu.VMEM((1024, 512), F32),
            pltpu.VMEM((1024, 1024), BF16), pltpu.VMEM((1024, 1024), BF16),
            pltpu.VMEM((1024, 512), BF16), pltpu.VMEM((1024, 512), BF16),
            pltpu.VMEM((1024, 512), BF16), pltpu.VMEM((1024, 512), BF16),
            pltpu.VMEM((1024, 512), F32), pltpu.VMEM((1024, 512), F32), pltpu.VMEM((384, 512), F32),
            pltpu.SemaphoreType.DMA((2, 4)),
            *buffers(256), *buffers(256),
            pltpu.VMEM((192, 512), F32), pltpu.VMEM((15, 48, 128), F32), pltpu.VMEM((4, 48, 128), F32),
            pltpu.SemaphoreType.DMA((151,)), pltpu.SemaphoreType.DMA((151,)), pltpu.SemaphoreType.DMA((1,)),
            pltpu.SemaphoreType.DMA((3,)),
        ],
        compiler_params=pltpu.CompilerParams(
            collective_id=0, has_side_effects=True, vmem_limit_bytes=60 * 2**20),
    )(block, basis)


def eliminate(t):
    sub = lax.broadcasted_iota(jnp.int32, (8, 128), 0)
    lane = lax.broadcasted_iota(jnp.int32, (8, 128), 1)

    def row(v, j):
        return jnp.broadcast_to(v[j : j + 1, :], (8, 128))

    def col(v, c):
        return jnp.broadcast_to(v[:, c : c + 1], (8, 128))

    def update(i, lo, zr):
        a0 = t[8 * i : 8 * i + 8, 0:128]
        a1 = t[8 * i : 8 * i + 8, 128:256]
        ci = [col(a0, lo + k) for k in range(8)]
        s0 = [ci[k] * zr[k][0] for k in range(8)]
        s1 = [ci[k] * zr[k][1] for k in range(8)]
        while len(s0) > 1:
            s0 = [s0[x] + s0[x + 1] for x in range(0, len(s0), 2)]
            s1 = [s1[x] + s1[x + 1] for x in range(0, len(s1), 2)]
        v0, v1 = a0 - s0[0], a1 - s1[0]
        t[8 * i : 8 * i + 8, 0:128] = v0
        t[8 * i : 8 * i + 8, 128:256] = v1
        return v0, v1

    v0, v1 = t[0:8, 0:128], t[0:8, 128:256]
    for p in range(16):
        lo = 8 * p
        x = [col(v0, lo + k) for k in range(8)] + [v0, v1]
        raw0, raw1 = v0, v1
        a_of = jnp.ones((8, 128), F32)
        b_of = jnp.zeros((8, 128), F32)
        d_of = b_of
        for j in range(0, 8, 2):
            even, odd = sub == j, sub == j + 1
            pair = even | odd
            top = [row(v, j) if n > j else None for n, v in enumerate(x)]
            low = [row(v, j + 1) if n > j else None for n, v in enumerate(x)]
            a, b, c = row(x[j], j), top[j + 1], low[j + 1]
            g = 1.0 / (a * c - b * b)
            n0 = jnp.where(even, c, jnp.where(odd, -b, x[j + 1] * b - x[j] * c))
            n1 = jnp.where(even, -b, jnp.where(odd, a, x[j] * b - x[j + 1] * a))
            raw0 = jnp.where(even, top[8], jnp.where(odd, low[8], raw0))
            raw1 = jnp.where(even, top[9], jnp.where(odd, low[9], raw1))
            a_of = jnp.where(odd, a, a_of)
            b_of = jnp.where(odd, b, b_of)
            d_of = jnp.where(even, a, jnp.where(odd, c, d_of))
            for n in range(j + 2, 10):
                x[n] = jnp.where(pair, 0.0, x[n]) + g * (n0 * top[n] + n1 * low[n])
        zr = [(row(x[8], k), row(x[9], k)) for k in range(8)]
        if p < 15:
            v0, v1 = update(p + 1, lo, zr)
        m = b_of / a_of
        q = 1.0 / jnp.sqrt(d_of - m * b_of)
        u0 = raw0 - m * pltpu.roll(raw0, 1, 0)
        u1 = raw1 - m * pltpu.roll(raw1, 1, 0)
        t[lo : lo + 8, 0:128] = jnp.where(lane >= sub + lo, u0 * q, 0.0)
        t[lo : lo + 8, 128:256] = u1 * q
        for i in range(p + 2, 16):
            update(i, lo, zr)


def exact(a, b, dims):
    return lax.dot_general(a, b, (dims, ((), ())), precision=HI, preferred_element_type=F32)


def factor_kernel(g_in, ph_in, pl_in, coeffs, ortho_out, r_out, coeffs_out, g, ph, pl_, kept, ortho, r, s, t, w, root, sems):
    copies = [pltpu.make_async_copy(a, b, sems.at[i]) for i, (a, b) in enumerate(
        ((g_in, g), (ph_in, ph), (pl_in, pl_), (coeffs, kept)))]
    for copy in copies:
        copy.start()
    n = 512
    r[...] = jnp.zeros((n, n), F32)
    w[...] = jnp.zeros((n, n), F32)
    s[:, n : 2 * n] = jnp.zeros((n, n), F32)
    eye = lax.broadcasted_iota(jnp.int32, (128, 128), 0) == lax.broadcasted_iota(jnp.int32, (128, 128), 1)
    copies[0].wait()
    s[0:256, 0:n] = g[0:256, :]
    s[256:384, 256:n] = g[256:384, 0:256]
    s[384:512, 256:n] = g[256:384, 256:n]
    down = []
    for b in range(4):
        at = slice(b * 128, b * 128 + 128)
        diagonal = jnp.where(eye, s[at, at], 0.0)
        across = jnp.sqrt(jnp.sum(diagonal, axis=0, keepdims=True))
        root[0:1, at] = across
        root[1:2, at] = 1.0 / across
        s[at, n + b * 128 : n + b * 128 + 128] = jnp.where(eye, 1.0 / across, 0.0)
        down.append(1.0 / jnp.sqrt(jnp.sum(diagonal, axis=1, keepdims=True)))
    for b in range(4):
        at = slice(b * 128, b * 128 + 128)
        s[at, b * 128 : n] = s[at, b * 128 : n] * down[b] * root[1:2, b * 128 : n]

    def body(step, carry):
        for b in range(4):
            @pl.when(step == b)
            def _():
                t[:, 0:128] = s[b * 128 : b * 128 + 128, b * 128 : b * 128 + 128]
                t[:, 128:256] = s[b * 128 : b * 128 + 128, n + b * 128 : n + b * 128 + 128]
        eliminate(t)
        for b in range(4):
            @pl.when(step == b)
            def _():
                lo, hi = b * 128, b * 128 + 128
                scaled = t[:, 128:256]
                li = scaled * root[0:1, lo:hi]
                r[lo:hi, lo:hi] = t[:, 0:128] * root[0:1, lo:hi]
                w[lo:hi, lo:hi] = scaled
                if b:
                    w[lo:hi, 0:lo] = exact(li, s[lo:hi, n : n + lo], NN)
                if b < 3:
                    right = exact(li, s[lo:hi, hi:n], NN)
                    r[lo:hi, hi:n] = right * root[0:1, hi:n]
                    for c in range(b + 1, 4):
                        at = slice(c * 128, c * 128 + 128)
                        rc = right[:, (c - b - 1) * 128 : (c - b) * 128]
                        s[at, c * 128 : n] -= exact(rc, right[:, (c - b - 1) * 128 :], TN)
                        s[at, n : n + hi] -= exact(rc, w[lo:hi, 0:hi], TN)
        return carry

    copies[3].wait()
    stores = [pltpu.make_async_copy(kept, coeffs_out, sems.at[9])]
    stores[0].start()
    lax.fori_loop(0, 4, body, 0)
    stores.append(pltpu.make_async_copy(r, r_out, sems.at[4]))
    stores[1].start()
    copies[1].wait()
    copies[2].wait()
    wh, wl = split(w[...])
    for i in range(4):
        rows = slice(i * 256, i * 256 + 256)
        for c in range(2):
            at, k = slice(c * 256, c * 256 + 256), slice(0, c * 256 + 256)
            ortho[rows, at] = dot3(ph[rows, k], pl_[rows, k], wh[at, k], wl[at, k], NT)
        stores.append(pltpu.make_async_copy(ortho.at[pl.ds(i * 256, 256)], ortho_out.at[pl.ds(i * 256, 256)], sems.at[5 + i]))
        stores[-1].start()
    for copy in stores:
        copy.wait()


def orthogonalize(gram, ph, pl_, coeffs):
    anywhere = pl.BlockSpec(memory_space=pl.ANY)
    return pl.pallas_call(
        factor_kernel,
        out_shape=[
            jax.ShapeDtypeStruct((1024, 512), F32), jax.ShapeDtypeStruct((512, 512), F32),
            jax.ShapeDtypeStruct((1024, 512), F32),
        ],
        in_specs=[anywhere] * 4,
        out_specs=[anywhere] * 3,
        scratch_shapes=[
            pltpu.VMEM((384, 512), F32), pltpu.VMEM((1024, 512), BF16), pltpu.VMEM((1024, 512), BF16),
            pltpu.VMEM((1024, 512), F32), pltpu.VMEM((1024, 512), F32), pltpu.VMEM((512, 512), F32),
            pltpu.VMEM((512, 1024), F32), pltpu.VMEM((128, 256), F32), pltpu.VMEM((512, 512), F32),
            pltpu.VMEM((8, 512), F32), pltpu.SemaphoreType.DMA((10,)),
        ],
        compiler_params=pltpu.CompilerParams(vmem_limit_bytes=63 * 2**20),
    )(gram, ph, pl_, coeffs)


def shards(block, basis):
    rows_total = block.shape[0] * lax.axis_size("leaf") * lax.axis_size("side")
    ph, pl_, gram, coeffs = project(block, basis, rows_total)
    return orthogonalize(gram, ph, pl_, coeffs)


def solution(mesh):
    return jax.shard_map(
        shards,
        mesh=mesh,
        in_specs=(P(("leaf", "side"), None), P(("leaf", "side"), None)),
        out_specs=(P(("leaf", "side"), None), P(), P()),
        check_vma=False,
    )
```

```python
import functools
import jax
import jax.numpy as jnp
from jax import lax
from jax.experimental import pallas as pl
from jax.experimental.pallas import tpu as pltpu
from jax.sharding import PartitionSpec as P

F32 = jnp.float32
BF16 = jnp.bfloat16
MESH = pl.DeviceIdType.MESH
HI = lax.Precision.HIGHEST
AXES = ((0, 1, 2), (1, 2, 0), (2, 0, 1))


def position():
    leaf, side = lax.axis_index("leaf"), lax.axis_index("side")
    return [leaf // 4, lax.rem(leaf, 4), side // 2], lax.rem(side, 2)


def device(q, core):
    return (q[0] * 4 + q[1], q[2] * 2 + core)


def peer(q, core, axis, k, second=None, k2=0):
    to = list(q)
    to[axis] = lax.rem(q[axis] + k, 4)
    if second is not None:
        to[second] = lax.rem(q[second] + k2, 4)
    return device(to, core)


def split(v):
    hi = v.astype(BF16)
    return hi, (v - hi.astype(F32)).astype(BF16)


def dot(a, b, dims):
    return lax.dot_general(a, b, (dims, ((), ())), preferred_element_type=F32)


NN, TN, NT = ((1,), (0,)), ((0,), (0,)), ((1,), (1,))


def dot3(ah, al, bh, bl, dims):
    return dot(ah, bh, dims) + (dot(ah, bl, dims) + dot(al, bh, dims))


class Sum:
    def __init__(self, half, stride, base, streams, x, out, halves, a, y, b, c, send, recv):
        self.half, self.streams, self.x, self.out = half, streams, x, out
        self.halves, self.a, self.y, self.b, self.c = halves, a, y, b, c
        self.send, self.recv = send, recv
        self.q, self.core = position()
        self.mine = self.core * stride + base
        self.other = (1 - self.core) * stride + base
        self.pending = []

    def copy(self, src, dst, slot, to):
        return pltpu.make_async_remote_copy(
            src_ref=src, dst_ref=dst, send_sem=self.send.at[slot], recv_sem=self.recv.at[slot],
            device_id=to, device_id_type=MESH)

    def start(self, src, dst, slot, to):
        copy = self.copy(src, dst, slot, to)
        copy.start()
        self.pending.append(copy)

    def arrive(self, ref, slot):
        self.copy(ref, ref, slot, device(self.q, 1 - self.core)).wait_recv()

    def rows(self, at, n):
        return pl.ds(pl.multiple_of(at, 8), n)

    def give(self):
        chunk, off, n = 0, 0, self.half
        src = self.x.at[self.rows(self.other + off, n)]
        self.start(src, self.halves.at[pl.ds(off, n)], chunk, device(self.q, 1 - self.core))

    def take(self):
        chunk, off, n = 0, 0, self.half
        self.arrive(self.halves.at[pl.ds(off, n)], chunk)
        at = self.rows(self.mine + off, n)
        self.x[at, :] += self.halves[pl.ds(off, n), :]

    def slot(self, phase, s, k):
        return 4 + phase * 9 + s * 3 + k - 1

    def phase_a(self, s):
        off, n = self.streams[s]
        axis = AXES[s][0]
        for k in (2, 1, 3):
            part = lax.rem(self.q[axis] + k, 4)
            src = self.x.at[self.rows(self.mine + off + part * (n // 4), n // 4)]
            dst = self.a.at[k - 1, pl.ds(off // 4, n // 4)]
            self.start(src, dst, self.slot(0, s, k), peer(self.q, self.core, axis, k))

    def phase_b(self, s):
        off, n = self.streams[s]
        axis, nxt = AXES[s][0], AXES[s][1]
        at = pl.ds(off // 4, n // 4)
        for k in (1, 3, 2):
            self.arrive(self.a.at[k - 1, at], self.slot(0, s, k))
        own = self.x[self.rows(self.mine + off + self.q[axis] * (n // 4), n // 4), :]
        self.y[at, :] = (own + self.a[0, at, :]) + (self.a[1, at, :] + self.a[2, at, :])
        for k in (2, 1, 3):
            part = lax.rem(self.q[nxt] + k, 4)
            src = self.y.at[at, pl.ds(pl.multiple_of(part * 128, 128), 128)]
            self.start(src, self.b.at[k - 1, at], self.slot(1, s, k), peer(self.q, self.core, nxt, k))

    def phase_c(self, s):
        off, n = self.streams[s]
        axis, nxt = AXES[s][1], AXES[s][2]
        at = pl.ds(off // 4, n // 4)
        for k in (1, 3, 2):
            self.arrive(self.b.at[k - 1, at], self.slot(1, s, k))
        own = self.y[at, pl.ds(pl.multiple_of(self.q[axis] * 128, 128), 128)]
        me = self.q[nxt]
        self.c[me, at, :] = (own + self.b[0, at, :]) + (self.b[1, at, :] + self.b[2, at, :])
        for k in (2, 1, 3):
            self.start(self.c.at[me, at], self.c.at[me, at], self.slot(2, s, k), peer(self.q, self.core, nxt, k))

    def quarter(self, s, part):
        off, n = self.streams[s]
        return self.rows(self.mine + off + part * (n // 4), n // 4)

    def phase_d(self, s):
        off, n = self.streams[s]
        second, third = AXES[s][1], AXES[s][2]
        at = pl.ds(off // 4, n // 4)
        for k in (1, 3, 2):
            self.arrive(self.c.at[lax.rem(self.q[third] + 4 - k, 4), at], self.slot(2, s, k))
        rows = self.quarter(s, self.q[AXES[s][0]])
        columns = pl.ds(pl.multiple_of(self.q[second] * 128, 128), 128)
        self.out[rows, columns] = (self.c[0, at, :] + self.c[1, at, :]) + (self.c[2, at, :] + self.c[3, at, :])
        for k in (2, 1, 3):
            block = self.out.at[rows, columns]
            self.start(block, block, self.slot(3, s, k), peer(self.q, self.core, second, k))

    def phase_e(self, s):
        first, second = AXES[s][0], AXES[s][1]
        rows = self.quarter(s, self.q[first])
        for k in (1, 3, 2):
            part = lax.rem(self.q[second] + 4 - k, 4)
            columns = pl.ds(pl.multiple_of(part * 128, 128), 128)
            self.arrive(self.out.at[rows, columns], self.slot(3, s, k))
        for k in (2, 1, 3):
            self.start(self.out.at[rows], self.out.at[rows], self.slot(4, s, k), peer(self.q, self.core, first, k))
        self.start(self.out.at[rows], self.out.at[rows], 49 + s * 4, device(self.q, 1 - self.core))

    def phase_f(self, s, ks):
        first = AXES[s][0]
        for k in ks:
            rows = self.quarter(s, lax.rem(self.q[first] + 4 - k, 4))
            self.arrive(self.out.at[rows], self.slot(4, s, k))
            self.start(self.out.at[rows], self.out.at[rows], 49 + s * 4 + k, device(self.q, 1 - self.core))

    def meet(self):
        for s, (off, n) in enumerate(self.streams):
            for k in range(4):
                part = lax.rem(self.q[AXES[s][0]] + 4 - k, 4)
                self.arrive(self.out.at[self.rows(self.other + off + part * (n // 4), n // 4)], 49 + s * 4 + k)

    def drain(self):
        for copy in self.pending:
            copy.wait_send()


class PlaneSum(Sum):
    def plane(self, gather, s, k, k2):
        return 61 + gather * 45 + s * 15 + k * 4 + k2 - 1

    def scatter(self, s):
        off, n = self.streams[s]
        first, second = AXES[s][0], AXES[s][1]
        at = pl.ds(off // 4, n // 4)
        for k, k2 in STEPS:
            rows = self.quarter(s, lax.rem(self.q[first] + k, 4), self.x)
            columns = self.columns(lax.rem(self.q[second] + k2, 4))
            self.start(self.x.at[rows, columns], self.b.at[k * 4 + k2 - 1, at], self.plane(0, s, k, k2),
                       peer(self.q, self.core, first, k, second, k2))

    def columns(self, part):
        return pl.ds(pl.multiple_of(part * 128, 128), 128)

    def quarter(self, s, part, ref=None):
        off, n = self.streams[s]
        return self.rows(self.mine + off + part * (n // 4), n // 4)

    def exchange(self, s):
        off, n = self.streams[s]
        first, second, third = AXES[s]
        at = pl.ds(off // 4, n // 4)
        for k, k2 in STEPS[::-1]:
            self.arrive(self.b.at[k * 4 + k2 - 1, at], self.plane(0, s, k, k2))
        parts = [self.b[i, at, :] for i in range(15)]
        parts.append(self.x[self.quarter(s, self.q[first]), self.columns(self.q[second])])
        while len(parts) > 1:
            parts = [parts[i] + parts[i + 1] for i in range(0, len(parts), 2)]
        me = self.q[third]
        self.c[me, at, :] = parts[0]
        for k in (2, 1, 3):
            self.start(self.c.at[me, at], self.c.at[me, at], self.slot(2, s, k), peer(self.q, self.core, third, k))

    def gather(self, s):
        off, n = self.streams[s]
        first, second, third = AXES[s]
        at = pl.ds(off // 4, n // 4)
        for k in (1, 3, 2):
            self.arrive(self.c.at[lax.rem(self.q[third] + 4 - k, 4), at], self.slot(2, s, k))
        block = self.out.at[self.quarter(s, self.q[first]), self.columns(self.q[second])]
        block[...] = (self.c[0, at, :] + self.c[1, at, :]) + (self.c[2, at, :] + self.c[3, at, :])
        for k, k2 in STEPS:
            self.start(block, block, self.plane(1, s, k, k2), peer(self.q, self.core, first, k, second, k2))

    def forward(self, s, ks):
        first, second = AXES[s][0], AXES[s][1]
        for k in ks:
            rows = self.quarter(s, lax.rem(self.q[first] + 4 - k, 4))
            for k2 in (0, 1, 3, 2):
                if k or k2:
                    block = self.out.at[rows, self.columns(lax.rem(self.q[second] + 4 - k2, 4))]
                    self.arrive(block, self.plane(1, s, k, k2))
            self.start(self.out.at[rows], self.out.at[rows], 49 + s * 4 + k, device(self.q, 1 - self.core))


STEPS = tuple((k, k2) for k in (2, 1, 3, 0) for k2 in (2, 1, 3, 0) if k or k2)


WIDE = ((0, 96), (96, 96), (192, 64))
SMALL = ((0, 64), (64, 64), (128, 64))


def project_kernel(scale, block_in, basis_in, ph_out, pl_out, gram, coeffs_out, bs, bk, sh, sl, kh, kl, ph, pl_, x1, coeffs, x2,
                   load, *rest):
    buffers0, buffers1, buffers2, store = rest[0:7], rest[7:14], rest[14:20], rest[20]
    q, core = position()
    loads = []
    for i in range(4):
        at = pl.ds(i * 256, 256)
        loads.append((pltpu.make_async_copy(basis_in.at[at], bs.at[at], load.at[0, i]),
                      pltpu.make_async_copy(block_in.at[at], bk.at[at], load.at[1, i])))
    for pair in loads:
        for copy in pair:
            copy.start()
    barrier = pltpu.get_barrier_semaphore()
    partners = [device(q, 1 - core)] + [peer(q, core, axis, k) for axis in range(3) for k in (1, 2, 3)]
    partners += [peer(q, core, first, k, second, k2) for first, second, _ in AXES for k in (1, 2, 3) for k2 in (1, 2, 3)]
    for to in partners:
        pl.semaphore_signal(barrier, inc=1, device_id=to, device_id_type=MESH)

    for i in range(4):
        for copy in loads[i]:
            copy.wait()

        @pl.loop(i * 2, i * 2 + 2)
        def _(j):
            at = pl.ds(pl.multiple_of(j * 128, 128), 128)
            hi, lo = split(bs[at, :])
            sh[at, :] = hi
            sl[at, :] = lo
            hi, lo = split(bk[at, :])
            kh[at, :] = hi
            kl[at, :] = lo

    def terms(at):
        columns = pl.ds(pl.multiple_of(at, 256), 256)
        x1[columns, :] = dot3(sh[:, columns], sl[:, columns], kh[...], kl[...], TN)

    sums = [Sum(256, 512, 256 * i, WIDE, x1, coeffs, *half) for i, half in enumerate((buffers0[:7], buffers1[:7]))]
    for i in range(2):
        terms((1 - core) * 512 + i * 256)
        if i == 0:
            pl.semaphore_wait(barrier, len(partners))
        sums[i].give()
    for i in range(2):
        terms(core * 512 + i * 256)
        sums[i].take()
        for s in range(3):
            sums[i].phase_a(s)
    for phase in ("phase_b", "phase_c", "phase_d", "phase_e"):
        for each in sums:
            for s in range(3):
                getattr(each, phase)(s)

    def subtract(at):
        rows = pl.ds(pl.multiple_of(at, 256), 256)
        hi, lo = split(coeffs[rows, :])
        kh[rows, :] = hi
        kl[rows, :] = lo

        @pl.loop(0, 4)
        def _(i):
            at = pl.ds(pl.multiple_of(i * 256, 256), 256)
            bk[at, :] -= dot3(sh[at, rows], sl[at, rows], kh[rows, :], kl[rows, :], NN)

    for i in range(2):
        for ks in ((1, 3), (2,)):
            for s in range(3):
                sums[i].phase_f(s, ks)
        subtract(core * 512 + i * 256)
    for i in range(2):
        sums[i].meet()
        subtract((1 - core) * 512 + i * 256)

    keep = [pltpu.make_async_copy(coeffs, coeffs_out, store.at[0])]
    keep[0].start()

    @pl.loop(0, 4)
    def _(i):
        at = pl.ds(pl.multiple_of(i * 256, 256), 256)
        hi, lo = split(bk[at, :])
        ph[at, :] = hi
        pl_[at, :] = lo

    keep += [pltpu.make_async_copy(ph, ph_out, store.at[1]), pltpu.make_async_copy(pl_, pl_out, store.at[2])]
    keep[1].start()
    keep[2].start()
    left = pl.ds(0, 256)
    right = pl.ds(256, 256)
    x2[0:256, :] = dot3(ph[:, left], pl_[:, left], ph[...], pl_[...], TN) * scale
    corner = dot3(ph[:, right], pl_[:, right], ph[:, right], pl_[:, right], TN) * scale
    x2[256:384, 0:256] = corner[0:128]
    x2[256:384, 256:512] = corner[128:256]
    halves, b, c, send, recv = buffers2[0], buffers2[1], buffers2[2], buffers2[3], buffers2[4]
    last = PlaneSum(192, 192, 0, SMALL, x2, gram, halves, None, None, b, c, send, recv)
    last.give()
    last.take()
    for phase in (last.scatter, last.exchange, last.gather):
        for s in range(3):
            phase(s)
    for ks in ((0, 1, 3), (2,)):
        for s in range(3):
            last.forward(s, ks)
    last.meet()
    for each in (*sums, last):
        each.drain()
    for copy in keep:
        copy.wait()


def buffers(half):
    return [
        pltpu.VMEM((half, 512), F32), pltpu.VMEM((3, half // 4, 512), F32), pltpu.VMEM((half // 4, 512), F32),
        pltpu.VMEM((3, half // 4, 128), F32), pltpu.VMEM((4, half // 4, 128), F32),
        pltpu.SemaphoreType.DMA((61,)), pltpu.SemaphoreType.DMA((61,)),
    ]


def project(block, basis, rows_total):
    anywhere = pl.BlockSpec(memory_space=pl.ANY)
    return pl.pallas_call(
        functools.partial(project_kernel, 1.0 / rows_total),
        out_shape=[
            jax.ShapeDtypeStruct((1024, 512), BF16), jax.ShapeDtypeStruct((1024, 512), BF16),
            jax.ShapeDtypeStruct((384, 512), F32), jax.ShapeDtypeStruct((1024, 512), F32),
        ],
        in_specs=[anywhere] * 2,
        out_specs=[anywhere, anywhere, pl.BlockSpec(memory_space=pltpu.VMEM), anywhere],
        scratch_shapes=[
            pltpu.VMEM((1024, 1024), F32), pltpu.VMEM((1024, 512), F32),
            pltpu.VMEM((1024, 1024), BF16), pltpu.VMEM((1024, 1024), BF16),
            pltpu.VMEM((1024, 512), BF16), pltpu.VMEM((1024, 512), BF16),
            pltpu.VMEM((1024, 512), BF16), pltpu.VMEM((1024, 512), BF16),
            pltpu.VMEM((1024, 512), F32), pltpu.VMEM((1024, 512), F32), pltpu.VMEM((384, 512), F32),
            pltpu.SemaphoreType.DMA((2, 4)),
            *buffers(256), *buffers(256),
            pltpu.VMEM((192, 512), F32), pltpu.VMEM((15, 48, 128), F32), pltpu.VMEM((4, 48, 128), F32),
            pltpu.SemaphoreType.DMA((151,)), pltpu.SemaphoreType.DMA((151,)), pltpu.SemaphoreType.DMA((1,)),
            pltpu.SemaphoreType.DMA((3,)),
        ],
        compiler_params=pltpu.CompilerParams(
            collective_id=0, has_side_effects=True, vmem_limit_bytes=60 * 2**20),
    )(block, basis)


def eliminate(t):
    sub = lax.broadcasted_iota(jnp.int32, (8, 128), 0)
    lane = lax.broadcasted_iota(jnp.int32, (8, 128), 1)

    def row(v, j):
        return jnp.broadcast_to(v[j : j + 1, :], (8, 128))

    def col(v, c):
        return jnp.broadcast_to(v[:, c : c + 1], (8, 128))

    def total(terms):
        while len(terms) > 1:
            terms = [terms[i] + terms[i + 1] for i in range(0, len(terms), 2)]
        return terms[0]

    def stack(v, order):
        h = v.astype(BF16).astype(F32)
        m = (v - h).astype(BF16).astype(F32)
        three = h, m, v - h - m
        return jnp.concatenate([three[i] for i in order], axis=0).astype(BF16)

    def solve(x, v0, v1, lo):
        x = x + [v0, v1]
        raw0, raw1 = v0, v1
        end = len(x)
        a_of = jnp.ones((8, 128), F32)
        b_of = d_of = jnp.zeros((8, 128), F32)
        for j in range(0, 8, 2):
            even, odd = sub == j, sub == j + 1
            pair = even | odd
            top = [row(v, j) if n > j else None for n, v in enumerate(x)]
            low = [row(v, j + 1) if n > j else None for n, v in enumerate(x)]
            a, b, c = row(x[j], j), top[j + 1], low[j + 1]
            g = 1.0 / (a * c - b * b)
            n0 = jnp.where(even, c, jnp.where(odd, -b, x[j + 1] * b - x[j] * c))
            n1 = jnp.where(even, -b, jnp.where(odd, a, x[j] * b - x[j + 1] * a))
            raw0 = jnp.where(even, top[end - 2], jnp.where(odd, low[end - 2], raw0))
            raw1 = jnp.where(even, top[end - 1], jnp.where(odd, low[end - 1], raw1))
            a_of = jnp.where(odd, a, a_of)
            b_of = jnp.where(odd, b, b_of)
            d_of = jnp.where(even, a, jnp.where(odd, c, d_of))
            for n in range(j + 2, end):
                x[n] = jnp.where(pair, 0.0, x[n]) + g * (n0 * top[n] + n1 * low[n])
        m = b_of / a_of
        q = 1.0 / jnp.sqrt(d_of - m * b_of)
        u0 = raw0 - m * pltpu.roll(raw0, 1, 0)
        u1 = raw1 - m * pltpu.roll(raw1, 1, 0)
        t[lo : lo + 8, 0:128] = jnp.where(lane >= sub + lo, u0 * q, 0.0)
        t[lo : lo + 8, 128:256] = u1 * q
        return x

    now = [(t[i : i + 8, 0:128], t[i : i + 8, 128:256]) for i in (0, 8)]
    for p in range(8):
        lo = 16 * p
        (a0, a1), (b0, b1) = now
        own = [col(a0, lo + k) for k in range(8)]
        across = [col(a0, lo + 8 + k) for k in range(8)]
        down = [col(b0, lo + k) for k in range(8)]
        corner = [col(b0, lo + 8 + k) for k in range(8)]
        x = solve(own + across, a0, a1, lo)
        across, y0, y1 = x[8:16], x[16], x[17]
        corner = [corner[k] - total([down[m] * row(across[k], m) for m in range(8)]) for k in range(8)]
        c0 = b0 - total([down[m] * row(y0, m) for m in range(8)])
        c1 = b1 - total([down[m] * row(y1, m) for m in range(8)])
        x = solve(corner, c0, c1, lo + 8)
        z0, z1 = x[8], x[9]
        if p == 7:
            break
        y0 = y0 - total([across[k] * row(z0, k) for k in range(8)])
        y1 = y1 - total([across[k] * row(z1, k) for k in range(8)])
        now = []
        for i in (lo + 16, lo + 24):
            v0, v1 = t[i : i + 8, 0:128], t[i : i + 8, 128:256]
            ci = [col(v0, lo + k) for k in range(16)]
            now.append((v0 - total([ci[k] * row((y0, z0)[k // 8], k % 8) for k in range(16)]),
                        v1 - total([ci[k] * row((y1, z1)[k // 8], k % 8) for k in range(16)])))
        if p < 6:
            left = stack(jnp.concatenate([a0, b0], axis=0), (0, 0, 1, 0, 2, 1))
            right = jnp.concatenate([jnp.concatenate([y0, y1], axis=1), jnp.concatenate([z0, z1], axis=1)], axis=0)
            change = lax.dot_general(left, stack(right, (0, 1, 0, 2, 0, 1)), (((0,), (0,)), ((), ())), preferred_element_type=F32)
            t[lo + 32 :, :] -= change[lo + 32 :, :]


def exact(a, b, dims):
    return lax.dot_general(a, b, (dims, ((), ())), precision=HI, preferred_element_type=F32)


def factor_kernel(g_in, ph_in, pl_in, coeffs, ortho_out, r_out, coeffs_out, g, ph, pl_, kept, ortho, r, s, t, w, root, sems):
    copies = [pltpu.make_async_copy(a, b, sems.at[i]) for i, (a, b) in enumerate(
        ((g_in, g), (ph_in, ph), (pl_in, pl_), (coeffs, kept)))]
    copies[0].start()
    n = 512
    r[...] = jnp.zeros((n, n), F32)
    w[...] = jnp.zeros((n, n), F32)
    s[:, n : 2 * n] = jnp.zeros((n, n), F32)
    eye = lax.broadcasted_iota(jnp.int32, (128, 128), 0) == lax.broadcasted_iota(jnp.int32, (128, 128), 1)
    copies[0].wait()
    for copy in copies[1:]:
        copy.start()
    s[0:256, 0:n] = g[0:256, :]
    s[256:384, 256:n] = g[256:384, 0:256]
    s[384:512, 256:n] = g[256:384, 256:n]
    down = []
    for b in range(4):
        at = slice(b * 128, b * 128 + 128)
        diagonal = jnp.where(eye, s[at, at], 0.0)
        across = jnp.sqrt(jnp.sum(diagonal, axis=0, keepdims=True))
        root[0:1, at] = across
        root[1:2, at] = 1.0 / across
        s[at, n + b * 128 : n + b * 128 + 128] = jnp.where(eye, 1.0 / across, 0.0)
        down.append(1.0 / jnp.sqrt(jnp.sum(diagonal, axis=1, keepdims=True)))
    for b in range(4):
        at = slice(b * 128, b * 128 + 128)
        s[at, b * 128 : n] = s[at, b * 128 : n] * down[b] * root[1:2, b * 128 : n]

    def body(step, carry):
        for b in range(4):
            @pl.when(step == b)
            def _():
                t[:, 0:128] = s[b * 128 : b * 128 + 128, b * 128 : b * 128 + 128]
                t[:, 128:256] = s[b * 128 : b * 128 + 128, n + b * 128 : n + b * 128 + 128]
        eliminate(t)
        for b in range(4):
            @pl.when(step == b)
            def _():
                lo, hi = b * 128, b * 128 + 128
                scaled = t[:, 128:256]
                li = scaled * root[0:1, lo:hi]
                r[lo:hi, lo:hi] = t[:, 0:128] * root[0:1, lo:hi]
                w[lo:hi, lo:hi] = scaled
                if b:
                    w[lo:hi, 0:lo] = exact(li, s[lo:hi, n : n + lo], NN)
                if b < 3:
                    right = exact(li, s[lo:hi, hi:n], NN)
                    r[lo:hi, hi:n] = right * root[0:1, hi:n]
                    for c in range(b + 1, 4):
                        at = slice(c * 128, c * 128 + 128)
                        rc = right[:, (c - b - 1) * 128 : (c - b) * 128]
                        s[at, c * 128 : n] -= exact(rc, right[:, (c - b - 1) * 128 :], TN)
                        s[at, n : n + hi] -= exact(rc, w[lo:hi, 0:hi], TN)
        return carry

    lax.fori_loop(0, 2, body, 0)
    copies[3].wait()
    stores = [pltpu.make_async_copy(kept, coeffs_out, sems.at[9])]
    stores[0].start()
    lax.fori_loop(2, 4, body, 0)
    stores.append(pltpu.make_async_copy(r, r_out, sems.at[4]))
    stores[1].start()
    copies[1].wait()
    copies[2].wait()
    wh, wl = split(w[...])
    for i in range(4):
        rows = slice(i * 256, i * 256 + 256)
        for c in range(2):
            at, k = slice(c * 256, c * 256 + 256), slice(0, c * 256 + 256)
            ortho[rows, at] = dot3(ph[rows, k], pl_[rows, k], wh[at, k], wl[at, k], NT)
        stores.append(pltpu.make_async_copy(ortho.at[pl.ds(i * 256, 256)], ortho_out.at[pl.ds(i * 256, 256)], sems.at[5 + i]))
        stores[-1].start()
    for copy in stores:
        copy.wait()


def orthogonalize(gram, ph, pl_, coeffs):
    anywhere = pl.BlockSpec(memory_space=pl.ANY)
    return pl.pallas_call(
        factor_kernel,
        out_shape=[
            jax.ShapeDtypeStruct((1024, 512), F32), jax.ShapeDtypeStruct((512, 512), F32),
            jax.ShapeDtypeStruct((1024, 512), F32),
        ],
        in_specs=[anywhere] * 4,
        out_specs=[anywhere] * 3,
        scratch_shapes=[
            pltpu.VMEM((384, 512), F32), pltpu.VMEM((1024, 512), BF16), pltpu.VMEM((1024, 512), BF16),
            pltpu.VMEM((1024, 512), F32), pltpu.VMEM((1024, 512), F32), pltpu.VMEM((512, 512), F32),
            pltpu.VMEM((512, 1024), F32), pltpu.VMEM((128, 256), F32), pltpu.VMEM((512, 512), F32),
            pltpu.VMEM((8, 512), F32), pltpu.SemaphoreType.DMA((10,)),
        ],
        compiler_params=pltpu.CompilerParams(vmem_limit_bytes=63 * 2**20),
    )(gram, ph, pl_, coeffs)


def shards(block, basis):
    rows_total = block.shape[0] * lax.axis_size("leaf") * lax.axis_size("side")
    ph, pl_, gram, coeffs = project(block, basis, rows_total)
    return orthogonalize(gram, ph, pl_, coeffs)


def solution(mesh):
    return jax.shard_map(
        shards,
        mesh=mesh,
        in_specs=(P(("leaf", "side"), None), P(("leaf", "side"), None)),
        out_specs=(P(("leaf", "side"), None), P(), P()),
        check_vma=False,
    )
```

```python
import functools
import jax
import jax.numpy as jnp
from jax import lax
from jax.experimental import pallas as pl
from jax.experimental.pallas import tpu as pltpu
from jax.sharding import PartitionSpec as P

F32 = jnp.float32
BF16 = jnp.bfloat16
MESH = pl.DeviceIdType.MESH
AXES = ((0, 1, 2), (1, 2, 0), (2, 0, 1))


def position():
    leaf, side = lax.axis_index("leaf"), lax.axis_index("side")
    return [leaf // 4, lax.rem(leaf, 4), side // 2], lax.rem(side, 2)


def device(q, core):
    return (q[0] * 4 + q[1], q[2] * 2 + core)


def peer(q, core, axis, k, second=None, k2=0):
    to = list(q)
    to[axis] = lax.rem(q[axis] + k, 4)
    if second is not None:
        to[second] = lax.rem(q[second] + k2, 4)
    return device(to, core)


def split(v):
    hi = v.astype(BF16)
    return hi, (v - hi.astype(F32)).astype(BF16)


def dot(a, b, dims):
    return lax.dot_general(a, b, (dims, ((), ())), preferred_element_type=F32)


NN, TN, NT = ((1,), (0,)), ((0,), (0,)), ((1,), (1,))


def dot3(ah, al, bh, bl, dims):
    return dot(ah, bh, dims) + (dot(ah, bl, dims) + dot(al, bh, dims))


class Sum:
    def __init__(self, half, stride, base, streams, x, out, halves, a, y, b, c, send, recv):
        self.half, self.streams, self.x, self.out = half, streams, x, out
        self.halves, self.a, self.y, self.b, self.c = halves, a, y, b, c
        self.send, self.recv = send, recv
        self.q, self.core = position()
        self.mine = self.core * stride + base
        self.other = (1 - self.core) * stride + base
        self.pending = []

    def copy(self, src, dst, slot, to):
        return pltpu.make_async_remote_copy(
            src_ref=src, dst_ref=dst, send_sem=self.send.at[slot], recv_sem=self.recv.at[slot],
            device_id=to, device_id_type=MESH)

    def start(self, src, dst, slot, to):
        copy = self.copy(src, dst, slot, to)
        copy.start()
        self.pending.append(copy)

    def arrive(self, ref, slot):
        self.copy(ref, ref, slot, device(self.q, 1 - self.core)).wait_recv()

    def rows(self, at, n):
        return pl.ds(pl.multiple_of(at, 8), n)

    def give(self):
        chunk, off, n = 0, 0, self.half
        src = self.x.at[self.rows(self.other + off, n)]
        self.start(src, self.halves.at[pl.ds(off, n)], chunk, device(self.q, 1 - self.core))

    def take(self):
        chunk, off, n = 0, 0, self.half
        self.arrive(self.halves.at[pl.ds(off, n)], chunk)
        at = self.rows(self.mine + off, n)
        self.x[at, :] += self.halves[pl.ds(off, n), :]

    def slot(self, phase, s, k):
        return 4 + phase * 9 + s * 3 + k - 1

    def phase_a(self, s):
        off, n = self.streams[s]
        axis = AXES[s][0]
        for k in (2, 1, 3):
            part = lax.rem(self.q[axis] + k, 4)
            src = self.x.at[self.rows(self.mine + off + part * (n // 4), n // 4)]
            dst = self.a.at[k - 1, pl.ds(off // 4, n // 4)]
            self.start(src, dst, self.slot(0, s, k), peer(self.q, self.core, axis, k))

    def phase_b(self, s):
        off, n = self.streams[s]
        axis, nxt = AXES[s][0], AXES[s][1]
        at = pl.ds(off // 4, n // 4)
        for k in (1, 3, 2):
            self.arrive(self.a.at[k - 1, at], self.slot(0, s, k))
        own = self.x[self.rows(self.mine + off + self.q[axis] * (n // 4), n // 4), :]
        self.y[at, :] = (own + self.a[0, at, :]) + (self.a[1, at, :] + self.a[2, at, :])
        for k in (2, 1, 3):
            part = lax.rem(self.q[nxt] + k, 4)
            src = self.y.at[at, pl.ds(pl.multiple_of(part * 128, 128), 128)]
            self.start(src, self.b.at[k - 1, at], self.slot(1, s, k), peer(self.q, self.core, nxt, k))

    def phase_c(self, s):
        off, n = self.streams[s]
        axis, nxt = AXES[s][1], AXES[s][2]
        at = pl.ds(off // 4, n // 4)
        for k in (1, 3, 2):
            self.arrive(self.b.at[k - 1, at], self.slot(1, s, k))
        own = self.y[at, pl.ds(pl.multiple_of(self.q[axis] * 128, 128), 128)]
        me = self.q[nxt]
        self.c[me, at, :] = (own + self.b[0, at, :]) + (self.b[1, at, :] + self.b[2, at, :])
        for k in (2, 1, 3):
            self.start(self.c.at[me, at], self.c.at[me, at], self.slot(2, s, k), peer(self.q, self.core, nxt, k))

    def quarter(self, s, part):
        off, n = self.streams[s]
        return self.rows(self.mine + off + part * (n // 4), n // 4)

    def phase_d(self, s):
        off, n = self.streams[s]
        second, third = AXES[s][1], AXES[s][2]
        at = pl.ds(off // 4, n // 4)
        for k in (1, 3, 2):
            self.arrive(self.c.at[lax.rem(self.q[third] + 4 - k, 4), at], self.slot(2, s, k))
        rows = self.quarter(s, self.q[AXES[s][0]])
        columns = pl.ds(pl.multiple_of(self.q[second] * 128, 128), 128)
        self.out[rows, columns] = (self.c[0, at, :] + self.c[1, at, :]) + (self.c[2, at, :] + self.c[3, at, :])
        for k in (2, 1, 3):
            block = self.out.at[rows, columns]
            self.start(block, block, self.slot(3, s, k), peer(self.q, self.core, second, k))

    def phase_e(self, s):
        first, second = AXES[s][0], AXES[s][1]
        rows = self.quarter(s, self.q[first])
        for k in (1, 3, 2):
            part = lax.rem(self.q[second] + 4 - k, 4)
            columns = pl.ds(pl.multiple_of(part * 128, 128), 128)
            self.arrive(self.out.at[rows, columns], self.slot(3, s, k))
        for k in (2, 1, 3):
            self.start(self.out.at[rows], self.out.at[rows], self.slot(4, s, k), peer(self.q, self.core, first, k))
        self.start(self.out.at[rows], self.out.at[rows], 49 + s * 4, device(self.q, 1 - self.core))

    def phase_f(self, s, ks):
        first = AXES[s][0]
        for k in ks:
            rows = self.quarter(s, lax.rem(self.q[first] + 4 - k, 4))
            self.arrive(self.out.at[rows], self.slot(4, s, k))
            self.start(self.out.at[rows], self.out.at[rows], 49 + s * 4 + k, device(self.q, 1 - self.core))

    def meet(self):
        for s, (off, n) in enumerate(self.streams):
            for k in range(4):
                part = lax.rem(self.q[AXES[s][0]] + 4 - k, 4)
                self.arrive(self.out.at[self.rows(self.other + off + part * (n // 4), n // 4)], 49 + s * 4 + k)

    def drain(self):
        for copy in self.pending:
            copy.wait_send()


class PlaneSum(Sum):
    def plane(self, gather, s, k, k2):
        return 61 + gather * 45 + s * 15 + k * 4 + k2 - 1

    def scatter(self, s):
        off, n = self.streams[s]
        first, second = AXES[s][0], AXES[s][1]
        at = pl.ds(off // 4, n // 4)
        for k, k2 in STEPS:
            rows = self.quarter(s, lax.rem(self.q[first] + k, 4), self.x)
            columns = self.columns(lax.rem(self.q[second] + k2, 4))
            self.start(self.x.at[rows, columns], self.b.at[k * 4 + k2 - 1, at], self.plane(0, s, k, k2),
                       peer(self.q, self.core, first, k, second, k2))

    def columns(self, part):
        return pl.ds(pl.multiple_of(part * 128, 128), 128)

    def quarter(self, s, part, ref=None):
        off, n = self.streams[s]
        return self.rows(self.mine + off + part * (n // 4), n // 4)

    def exchange(self, s):
        off, n = self.streams[s]
        first, second, third = AXES[s]
        at = pl.ds(off // 4, n // 4)
        for k, k2 in STEPS[::-1]:
            self.arrive(self.b.at[k * 4 + k2 - 1, at], self.plane(0, s, k, k2))
        parts = [self.b[i, at, :] for i in range(15)]
        parts.append(self.x[self.quarter(s, self.q[first]), self.columns(self.q[second])])
        while len(parts) > 1:
            parts = [parts[i] + parts[i + 1] for i in range(0, len(parts), 2)]
        me = self.q[third]
        self.c[me, at, :] = parts[0]
        for k in (2, 1, 3):
            self.start(self.c.at[me, at], self.c.at[me, at], self.slot(2, s, k), peer(self.q, self.core, third, k))

    def gather(self, s):
        off, n = self.streams[s]
        first, second, third = AXES[s]
        at = pl.ds(off // 4, n // 4)
        for k in (1, 3, 2):
            self.arrive(self.c.at[lax.rem(self.q[third] + 4 - k, 4), at], self.slot(2, s, k))
        block = self.out.at[self.quarter(s, self.q[first]), self.columns(self.q[second])]
        block[...] = (self.c[0, at, :] + self.c[1, at, :]) + (self.c[2, at, :] + self.c[3, at, :])
        for k, k2 in STEPS:
            self.start(block, block, self.plane(1, s, k, k2), peer(self.q, self.core, first, k, second, k2))

    def forward(self, s, ks):
        first, second = AXES[s][0], AXES[s][1]
        for k in ks:
            rows = self.quarter(s, lax.rem(self.q[first] + 4 - k, 4))
            for k2 in (0, 1, 3, 2):
                if k or k2:
                    block = self.out.at[rows, self.columns(lax.rem(self.q[second] + 4 - k2, 4))]
                    self.arrive(block, self.plane(1, s, k, k2))
            self.start(self.out.at[rows], self.out.at[rows], 49 + s * 4 + k, device(self.q, 1 - self.core))


STEPS = tuple((k, k2) for k in (2, 1, 3, 0) for k2 in (2, 1, 3, 0) if k or k2)


WIDE = ((0, 96), (96, 96), (192, 64))
SMALL = ((0, 64), (64, 64), (128, 64))


def project_kernel(scale, block_in, basis_in, ph_out, pl_out, gram, coeffs_out, bs, bk, sh, sl, kh, kl, ph, pl_, x1, coeffs, x2,
                   load, *rest):
    buffers0, buffers1, buffers2, store = rest[0:7], rest[7:14], rest[14:20], rest[20]
    q, core = position()
    loads = []
    for i in range(4):
        at = pl.ds(i * 256, 256)
        loads.append((pltpu.make_async_copy(basis_in.at[at], bs.at[at], load.at[0, i]),
                      pltpu.make_async_copy(block_in.at[at], bk.at[at], load.at[1, i])))
    for pair in loads:
        for copy in pair:
            copy.start()
    barrier = pltpu.get_barrier_semaphore()
    partners = [device(q, 1 - core)] + [peer(q, core, axis, k) for axis in range(3) for k in (1, 2, 3)]
    partners += [peer(q, core, first, k, second, k2) for first, second, _ in AXES for k in (1, 2, 3) for k2 in (1, 2, 3)]
    for to in partners:
        pl.semaphore_signal(barrier, inc=1, device_id=to, device_id_type=MESH)

    for i in range(4):
        for copy in loads[i]:
            copy.wait()

        @pl.loop(i * 2, i * 2 + 2)
        def _(j):
            at = pl.ds(pl.multiple_of(j * 128, 128), 128)
            hi, lo = split(bs[at, :])
            sh[at, :] = hi
            sl[at, :] = lo
            hi, lo = split(bk[at, :])
            kh[at, :] = hi
            kl[at, :] = lo

    def terms(at):
        columns = pl.ds(pl.multiple_of(at, 256), 256)
        x1[columns, :] = dot3(sh[:, columns], sl[:, columns], kh[...], kl[...], TN)

    sums = [Sum(256, 512, 256 * i, WIDE, x1, coeffs, *half) for i, half in enumerate((buffers0[:7], buffers1[:7]))]
    for i in range(2):
        terms((1 - core) * 512 + i * 256)
        if i == 0:
            pl.semaphore_wait(barrier, len(partners))
        sums[i].give()
    for i in range(2):
        terms(core * 512 + i * 256)
        sums[i].take()
        for s in range(3):
            sums[i].phase_a(s)
    for phase in ("phase_b", "phase_c", "phase_d", "phase_e"):
        for each in sums:
            for s in range(3):
                getattr(each, phase)(s)

    def subtract(at):
        rows = pl.ds(pl.multiple_of(at, 256), 256)
        hi, lo = split(coeffs[rows, :])
        kh[rows, :] = hi
        kl[rows, :] = lo

        @pl.loop(0, 4)
        def _(i):
            at = pl.ds(pl.multiple_of(i * 256, 256), 256)
            bk[at, :] -= dot3(sh[at, rows], sl[at, rows], kh[rows, :], kl[rows, :], NN)

    for i in range(2):
        for ks in ((1, 3), (2,)):
            for s in range(3):
                sums[i].phase_f(s, ks)
        subtract(core * 512 + i * 256)
    for i in range(2):
        sums[i].meet()
        subtract((1 - core) * 512 + i * 256)

    keep = [pltpu.make_async_copy(coeffs, coeffs_out, store.at[0])]
    keep[0].start()

    @pl.loop(0, 4)
    def _(i):
        at = pl.ds(pl.multiple_of(i * 256, 256), 256)
        hi, lo = split(bk[at, :])
        ph[at, :] = hi
        pl_[at, :] = lo

    keep += [pltpu.make_async_copy(ph, ph_out, store.at[1]), pltpu.make_async_copy(pl_, pl_out, store.at[2])]
    keep[1].start()
    keep[2].start()
    left = pl.ds(0, 256)
    right = pl.ds(256, 256)
    x2[0:256, :] = dot3(ph[:, left], pl_[:, left], ph[...], pl_[...], TN) * scale
    corner = dot3(ph[:, right], pl_[:, right], ph[:, right], pl_[:, right], TN) * scale
    x2[256:384, 0:256] = corner[0:128]
    x2[256:384, 256:512] = corner[128:256]
    halves, b, c, send, recv = buffers2[0], buffers2[1], buffers2[2], buffers2[3], buffers2[4]
    last = PlaneSum(192, 192, 0, SMALL, x2, gram, halves, None, None, b, c, send, recv)
    last.give()
    last.take()
    for phase in (last.scatter, last.exchange, last.gather):
        for s in range(3):
            phase(s)
    for ks in ((0, 1, 3), (2,)):
        for s in range(3):
            last.forward(s, ks)
    last.meet()
    for each in (*sums, last):
        each.drain()
    for copy in keep:
        copy.wait()


def buffers(half):
    return [
        pltpu.VMEM((half, 512), F32), pltpu.VMEM((3, half // 4, 512), F32), pltpu.VMEM((half // 4, 512), F32),
        pltpu.VMEM((3, half // 4, 128), F32), pltpu.VMEM((4, half // 4, 128), F32),
        pltpu.SemaphoreType.DMA((61,)), pltpu.SemaphoreType.DMA((61,)),
    ]


def project(block, basis, rows_total):
    anywhere = pl.BlockSpec(memory_space=pl.ANY)
    return pl.pallas_call(
        functools.partial(project_kernel, 1.0 / rows_total),
        out_shape=[
            jax.ShapeDtypeStruct((1024, 512), BF16), jax.ShapeDtypeStruct((1024, 512), BF16),
            jax.ShapeDtypeStruct((384, 512), F32), jax.ShapeDtypeStruct((1024, 512), F32),
        ],
        in_specs=[anywhere] * 2,
        out_specs=[anywhere, anywhere, pl.BlockSpec(memory_space=pltpu.VMEM), anywhere],
        scratch_shapes=[
            pltpu.VMEM((1024, 1024), F32), pltpu.VMEM((1024, 512), F32),
            pltpu.VMEM((1024, 1024), BF16), pltpu.VMEM((1024, 1024), BF16),
            pltpu.VMEM((1024, 512), BF16), pltpu.VMEM((1024, 512), BF16),
            pltpu.VMEM((1024, 512), BF16), pltpu.VMEM((1024, 512), BF16),
            pltpu.VMEM((1024, 512), F32), pltpu.VMEM((1024, 512), F32), pltpu.VMEM((384, 512), F32),
            pltpu.SemaphoreType.DMA((2, 4)),
            *buffers(256), *buffers(256),
            pltpu.VMEM((192, 512), F32), pltpu.VMEM((15, 48, 128), F32), pltpu.VMEM((4, 48, 128), F32),
            pltpu.SemaphoreType.DMA((151,)), pltpu.SemaphoreType.DMA((151,)), pltpu.SemaphoreType.DMA((1,)),
            pltpu.SemaphoreType.DMA((3,)),
        ],
        compiler_params=pltpu.CompilerParams(
            collective_id=0, has_side_effects=True, vmem_limit_bytes=48 * 2**20),
    )(block, basis)


def eliminate(t):
    sub = lax.broadcasted_iota(jnp.int32, (8, 128), 0)
    lane = lax.broadcasted_iota(jnp.int32, (8, 128), 1)

    def row(v, j):
        return jnp.broadcast_to(v[j : j + 1, :], (8, 128))

    def col(v, c):
        return jnp.broadcast_to(v[:, c : c + 1], (8, 128))

    def total(terms):
        while len(terms) > 1:
            terms = [terms[i] + terms[i + 1] for i in range(0, len(terms), 2)]
        return terms[0]

    def stack(v, order):
        h = v.astype(BF16).astype(F32)
        m = (v - h).astype(BF16).astype(F32)
        three = h, m, v - h - m
        return jnp.concatenate([three[i] for i in order], axis=0).astype(BF16)

    def solve(x, v0, v1, lo):
        x = x + [v0, v1]
        raw0, raw1 = v0, v1
        end = len(x)
        a_of = jnp.ones((8, 128), F32)
        b_of = d_of = jnp.zeros((8, 128), F32)
        for j in range(0, 8, 2):
            even, odd = sub == j, sub == j + 1
            pair = even | odd
            top = [row(v, j) if n > j else None for n, v in enumerate(x)]
            low = [row(v, j + 1) if n > j else None for n, v in enumerate(x)]
            a, b, c = row(x[j], j), top[j + 1], low[j + 1]
            g = 1.0 / (a * c - b * b)
            n0 = jnp.where(even, c, jnp.where(odd, -b, x[j + 1] * b - x[j] * c))
            n1 = jnp.where(even, -b, jnp.where(odd, a, x[j] * b - x[j + 1] * a))
            raw0 = jnp.where(even, top[end - 2], jnp.where(odd, low[end - 2], raw0))
            raw1 = jnp.where(even, top[end - 1], jnp.where(odd, low[end - 1], raw1))
            a_of = jnp.where(odd, a, a_of)
            b_of = jnp.where(odd, b, b_of)
            d_of = jnp.where(even, a, jnp.where(odd, c, d_of))
            for n in range(j + 2, end):
                x[n] = jnp.where(pair, 0.0, x[n]) + g * (n0 * top[n] + n1 * low[n])
        m = b_of / a_of
        q = 1.0 / jnp.sqrt(d_of - m * b_of)
        u0 = raw0 - m * pltpu.roll(raw0, 1, 0)
        u1 = raw1 - m * pltpu.roll(raw1, 1, 0)
        t[lo : lo + 8, 0:128] = jnp.where(lane >= sub + lo, u0 * q, 0.0)
        t[lo : lo + 8, 128:256] = u1 * q
        return x

    now = [(t[i : i + 8, 0:128], t[i : i + 8, 128:256]) for i in (0, 8)]
    for p in range(8):
        lo = 16 * p
        (a0, a1), (b0, b1) = now
        own = [col(a0, lo + k) for k in range(8)]
        across = [col(a0, lo + 8 + k) for k in range(8)]
        down = [col(b0, lo + k) for k in range(8)]
        corner = [col(b0, lo + 8 + k) for k in range(8)]
        x = solve(own + across, a0, a1, lo)
        across, y0, y1 = x[8:16], x[16], x[17]
        corner = [corner[k] - total([down[m] * row(across[k], m) for m in range(8)]) for k in range(8)]
        c0 = b0 - total([down[m] * row(y0, m) for m in range(8)])
        c1 = b1 - total([down[m] * row(y1, m) for m in range(8)])
        x = solve(corner, c0, c1, lo + 8)
        z0, z1 = x[8], x[9]
        if p == 7:
            break
        y0 = y0 - total([across[k] * row(z0, k) for k in range(8)])
        y1 = y1 - total([across[k] * row(z1, k) for k in range(8)])
        now = []
        for i in (lo + 16, lo + 24):
            v0, v1 = t[i : i + 8, 0:128], t[i : i + 8, 128:256]
            ci = [col(v0, lo + k) for k in range(16)]
            now.append((v0 - total([ci[k] * row((y0, z0)[k // 8], k % 8) for k in range(16)]),
                        v1 - total([ci[k] * row((y1, z1)[k // 8], k % 8) for k in range(16)])))
        if p < 6:
            left = stack(jnp.concatenate([a0, b0], axis=0), (0, 0, 1, 0, 2, 1))
            right = jnp.concatenate([jnp.concatenate([y0, y1], axis=1), jnp.concatenate([z0, z1], axis=1)], axis=0)
            change = lax.dot_general(left, stack(right, (0, 1, 0, 2, 0, 1)), (((0,), (0,)), ((), ())), preferred_element_type=F32)
            t[lo + 32 :, :] -= change[lo + 32 :, :]


SECOND = (0, 1, 0, 2, 0, 1)


def parts(v, order, axis):
    h = v.astype(BF16).astype(F32)
    m = (v - h).astype(BF16).astype(F32)
    three = [each.astype(BF16) for each in (h, m, v - h - m)]
    return jnp.concatenate([three[i] for i in order], axis=axis)


def factor_kernel(g, ph, pl_, coeffs, ortho_out, r_out, coeffs_out, ortho, r, s, t, w, root, sems):
    stores = [pltpu.make_async_copy(coeffs, coeffs_out, sems.at[0])]
    stores[0].start()
    n = 512
    r[...] = jnp.zeros((n, n), F32)
    w[...] = jnp.zeros((n, n), F32)
    s[:, n : 2 * n] = jnp.zeros((n, n), F32)
    eye = lax.broadcasted_iota(jnp.int32, (128, 128), 0) == lax.broadcasted_iota(jnp.int32, (128, 128), 1)
    s[0:256, 0:n] = g[0:256, :]
    s[256:384, 256:n] = g[256:384, 0:256]
    s[384:512, 256:n] = g[256:384, 256:n]
    down = []
    for b in range(4):
        at = slice(b * 128, b * 128 + 128)
        diagonal = jnp.where(eye, s[at, at], 0.0)
        across = jnp.sqrt(jnp.sum(diagonal, axis=0, keepdims=True))
        root[0:1, at] = across
        root[1:2, at] = 1.0 / across
        s[at, n + b * 128 : n + b * 128 + 128] = jnp.where(eye, 1.0 / across, 0.0)
        down.append(1.0 / jnp.sqrt(jnp.sum(diagonal, axis=1, keepdims=True)))
    for b in range(4):
        at = slice(b * 128, b * 128 + 128)
        s[at, b * 128 : n] = s[at, b * 128 : n] * down[b] * root[1:2, b * 128 : n]

    def body(step, carry):
        for b in range(4):
            @pl.when(step == b)
            def _():
                t[:, 0:128] = s[b * 128 : b * 128 + 128, b * 128 : b * 128 + 128]
                t[:, 128:256] = s[b * 128 : b * 128 + 128, n + b * 128 : n + b * 128 + 128]
        eliminate(t)
        for b in range(4):
            @pl.when(step == b)
            def _():
                lo, hi = b * 128, b * 128 + 128
                scaled = t[:, 128:256]
                li = scaled * root[0:1, lo:hi]
                r[lo:hi, lo:hi] = t[:, 0:128] * root[0:1, lo:hi]
                w[lo:hi, lo:hi] = scaled
                left = parts(li, (0, 0, 1, 0, 2, 1), 1)
                if b:
                    w[lo:hi, 0:lo] = dot(left, parts(s[lo:hi, n : n + lo], SECOND, 0), NN)
                if b < 3:
                    right = dot(left, parts(s[lo:hi, hi:n], SECOND, 0), NN)
                    r[lo:hi, hi:n] = right * root[0:1, hi:n]
                    down = parts(right, (0, 0, 1, 0, 2, 1), 0)
                    across = parts(right, SECOND, 0)
                    inverse = parts(w[lo:hi, 0:hi], SECOND, 0)
                    for c in range(b + 1, 4):
                        at = slice(c * 128, c * 128 + 128)
                        first = (c - b - 1) * 128
                        rows = down[:, first : first + 128]
                        s[at, c * 128 : n] -= dot(rows, across[:, first:], TN)
                        s[at, n : n + hi] -= dot(rows, inverse, TN)
        return carry

    lax.fori_loop(0, 4, body, 0)
    stores.append(pltpu.make_async_copy(r, r_out, sems.at[1]))
    stores[1].start()
    wh, wl = split(w[...])
    for i in range(4):
        rows = slice(i * 256, i * 256 + 256)
        for c in range(2):
            at, k = slice(c * 256, c * 256 + 256), slice(0, c * 256 + 256)
            ortho[rows, at] = dot3(ph[rows, k], pl_[rows, k], wh[at, k], wl[at, k], NT)
        stores.append(pltpu.make_async_copy(ortho.at[pl.ds(i * 256, 256)], ortho_out.at[pl.ds(i * 256, 256)], sems.at[2 + i]))
        stores[-1].start()
    for copy in stores:
        copy.wait()


def orthogonalize(gram, ph, pl_, coeffs):
    anywhere = pl.BlockSpec(memory_space=pl.ANY)
    return pl.pallas_call(
        factor_kernel,
        out_shape=[
            jax.ShapeDtypeStruct((1024, 512), F32), jax.ShapeDtypeStruct((512, 512), F32),
            jax.ShapeDtypeStruct((1024, 512), F32),
        ],
        in_specs=[pl.BlockSpec(memory_space=pltpu.VMEM)] * 3 + [anywhere],
        out_specs=[anywhere] * 3,
        scratch_shapes=[
            pltpu.VMEM((1024, 512), F32), pltpu.VMEM((512, 512), F32),
            pltpu.VMEM((512, 1024), F32), pltpu.VMEM((128, 256), F32), pltpu.VMEM((512, 512), F32),
            pltpu.VMEM((8, 512), F32), pltpu.SemaphoreType.DMA((6,)),
        ],
        compiler_params=pltpu.CompilerParams(vmem_limit_bytes=40 * 2**20),
    )(gram, ph, pl_, coeffs)


def shards(block, basis):
    rows_total = block.shape[0] * lax.axis_size("leaf") * lax.axis_size("side")
    ph, pl_, gram, coeffs = project(block, basis, rows_total)
    return orthogonalize(gram, ph, pl_, coeffs)


def solution(mesh):
    return jax.shard_map(
        shards,
        mesh=mesh,
        in_specs=(P(("leaf", "side"), None), P(("leaf", "side"), None)),
        out_specs=(P(("leaf", "side"), None), P(), P()),
        check_vma=False,
    )
```

```python
import functools
import jax
import jax.numpy as jnp
from jax import lax
from jax.experimental import pallas as pl
from jax.experimental.pallas import tpu as pltpu
from jax.sharding import PartitionSpec as P

F32 = jnp.float32
BF16 = jnp.bfloat16
MESH = pl.DeviceIdType.MESH
AXES = ((0, 1, 2), (1, 2, 0), (2, 0, 1))


def position():
    leaf, side = lax.axis_index("leaf"), lax.axis_index("side")
    return [leaf // 4, lax.rem(leaf, 4), side // 2], lax.rem(side, 2)


def device(q, core):
    return (q[0] * 4 + q[1], q[2] * 2 + core)


def peer(q, core, axis, k, second=None, k2=0):
    to = list(q)
    to[axis] = lax.rem(q[axis] + k, 4)
    if second is not None:
        to[second] = lax.rem(q[second] + k2, 4)
    return device(to, core)


def split(v):
    hi = v.astype(BF16)
    return hi, (v - hi.astype(F32)).astype(BF16)


def dot(a, b, dims):
    return lax.dot_general(a, b, (dims, ((), ())), preferred_element_type=F32)


NN, TN, NT = ((1,), (0,)), ((0,), (0,)), ((1,), (1,))


def dot3(ah, al, bh, bl, dims):
    return dot(ah, bh, dims) + (dot(ah, bl, dims) + dot(al, bh, dims))


class Sum:
    def __init__(self, half, stride, base, streams, x, out, halves, a, y, b, c, send, recv):
        self.half, self.streams, self.x, self.out = half, streams, x, out
        self.halves, self.a, self.y, self.b, self.c = halves, a, y, b, c
        self.send, self.recv = send, recv
        self.q, self.core = position()
        self.mine = self.core * stride + base
        self.other = (1 - self.core) * stride + base
        self.pending = []

    def copy(self, src, dst, slot, to):
        return pltpu.make_async_remote_copy(
            src_ref=src, dst_ref=dst, send_sem=self.send.at[slot], recv_sem=self.recv.at[slot],
            device_id=to, device_id_type=MESH)

    def start(self, src, dst, slot, to):
        copy = self.copy(src, dst, slot, to)
        copy.start()
        self.pending.append(copy)

    def arrive(self, ref, slot):
        self.copy(ref, ref, slot, device(self.q, 1 - self.core)).wait_recv()

    def rows(self, at, n):
        return pl.ds(pl.multiple_of(at, 8), n)

    def give(self):
        chunk, off, n = 0, 0, self.half
        src = self.x.at[self.rows(self.other + off, n)]
        self.start(src, self.halves.at[pl.ds(off, n)], chunk, device(self.q, 1 - self.core))

    def take(self):
        chunk, off, n = 0, 0, self.half
        self.arrive(self.halves.at[pl.ds(off, n)], chunk)
        at = self.rows(self.mine + off, n)
        self.x[at, :] += self.halves[pl.ds(off, n), :]

    def slot(self, phase, s, k):
        return 4 + phase * 9 + s * 3 + k - 1

    def phase_a(self, s):
        off, n = self.streams[s]
        axis = AXES[s][0]
        for k in (2, 1, 3):
            part = lax.rem(self.q[axis] + k, 4)
            src = self.x.at[self.rows(self.mine + off + part * (n // 4), n // 4)]
            dst = self.a.at[k - 1, pl.ds(off // 4, n // 4)]
            self.start(src, dst, self.slot(0, s, k), peer(self.q, self.core, axis, k))

    def phase_b(self, s):
        off, n = self.streams[s]
        axis, nxt = AXES[s][0], AXES[s][1]
        at = pl.ds(off // 4, n // 4)
        for k in (1, 3, 2):
            self.arrive(self.a.at[k - 1, at], self.slot(0, s, k))
        own = self.x[self.rows(self.mine + off + self.q[axis] * (n // 4), n // 4), :]
        self.y[at, :] = (own + self.a[0, at, :]) + (self.a[1, at, :] + self.a[2, at, :])
        for k in (2, 1, 3):
            part = lax.rem(self.q[nxt] + k, 4)
            src = self.y.at[at, pl.ds(pl.multiple_of(part * 128, 128), 128)]
            self.start(src, self.b.at[k - 1, at], self.slot(1, s, k), peer(self.q, self.core, nxt, k))

    def phase_c(self, s):
        off, n = self.streams[s]
        axis, nxt = AXES[s][1], AXES[s][2]
        at = pl.ds(off // 4, n // 4)
        for k in (1, 3, 2):
            self.arrive(self.b.at[k - 1, at], self.slot(1, s, k))
        own = self.y[at, pl.ds(pl.multiple_of(self.q[axis] * 128, 128), 128)]
        me = self.q[nxt]
        self.c[me, at, :] = (own + self.b[0, at, :]) + (self.b[1, at, :] + self.b[2, at, :])
        for k in (2, 1, 3):
            self.start(self.c.at[me, at], self.c.at[me, at], self.slot(2, s, k), peer(self.q, self.core, nxt, k))

    def quarter(self, s, part):
        off, n = self.streams[s]
        return self.rows(self.mine + off + part * (n // 4), n // 4)

    def phase_d(self, s):
        off, n = self.streams[s]
        second, third = AXES[s][1], AXES[s][2]
        at = pl.ds(off // 4, n // 4)
        for k in (1, 3, 2):
            self.arrive(self.c.at[lax.rem(self.q[third] + 4 - k, 4), at], self.slot(2, s, k))
        rows = self.quarter(s, self.q[AXES[s][0]])
        columns = pl.ds(pl.multiple_of(self.q[second] * 128, 128), 128)
        self.out[rows, columns] = (self.c[0, at, :] + self.c[1, at, :]) + (self.c[2, at, :] + self.c[3, at, :])
        for k in (2, 1, 3):
            block = self.out.at[rows, columns]
            self.start(block, block, self.slot(3, s, k), peer(self.q, self.core, second, k))

    def phase_e(self, s):
        first, second = AXES[s][0], AXES[s][1]
        rows = self.quarter(s, self.q[first])
        for k in (1, 3, 2):
            part = lax.rem(self.q[second] + 4 - k, 4)
            columns = pl.ds(pl.multiple_of(part * 128, 128), 128)
            self.arrive(self.out.at[rows, columns], self.slot(3, s, k))
        for k in (2, 1, 3):
            self.start(self.out.at[rows], self.out.at[rows], self.slot(4, s, k), peer(self.q, self.core, first, k))
        self.start(self.out.at[rows], self.out.at[rows], 49 + s * 4, device(self.q, 1 - self.core))

    def phase_f(self, s, ks):
        first = AXES[s][0]
        for k in ks:
            rows = self.quarter(s, lax.rem(self.q[first] + 4 - k, 4))
            self.arrive(self.out.at[rows], self.slot(4, s, k))
            self.start(self.out.at[rows], self.out.at[rows], 49 + s * 4 + k, device(self.q, 1 - self.core))

    def meet(self):
        for s, (off, n) in enumerate(self.streams):
            for k in range(4):
                part = lax.rem(self.q[AXES[s][0]] + 4 - k, 4)
                self.arrive(self.out.at[self.rows(self.other + off + part * (n // 4), n // 4)], 49 + s * 4 + k)

    def drain(self):
        for copy in self.pending:
            copy.wait_send()


class PlaneSum(Sum):
    def plane(self, gather, s, k, k2):
        return 61 + gather * 45 + s * 15 + k * 4 + k2 - 1

    def scatter(self, s):
        off, n = self.streams[s]
        first, second = AXES[s][0], AXES[s][1]
        at = pl.ds(off // 4, n // 4)
        for k, k2 in STEPS:
            rows = self.quarter(s, lax.rem(self.q[first] + k, 4), self.x)
            columns = self.columns(lax.rem(self.q[second] + k2, 4))
            self.start(self.x.at[rows, columns], self.b.at[k * 4 + k2 - 1, at], self.plane(0, s, k, k2),
                       peer(self.q, self.core, first, k, second, k2))

    def columns(self, part):
        return pl.ds(pl.multiple_of(part * 128, 128), 128)

    def quarter(self, s, part, ref=None):
        off, n = self.streams[s]
        return self.rows(self.mine + off + part * (n // 4), n // 4)

    def exchange(self, s):
        off, n = self.streams[s]
        first, second, third = AXES[s]
        at = pl.ds(off // 4, n // 4)
        for k, k2 in STEPS[::-1]:
            self.arrive(self.b.at[k * 4 + k2 - 1, at], self.plane(0, s, k, k2))
        parts = [self.b[i, at, :] for i in range(15)]
        parts.append(self.x[self.quarter(s, self.q[first]), self.columns(self.q[second])])
        while len(parts) > 1:
            parts = [parts[i] + parts[i + 1] for i in range(0, len(parts), 2)]
        me = self.q[third]
        self.c[me, at, :] = parts[0]
        for k in (2, 1, 3):
            self.start(self.c.at[me, at], self.c.at[me, at], self.slot(2, s, k), peer(self.q, self.core, third, k))

    def gather(self, s):
        off, n = self.streams[s]
        first, second, third = AXES[s]
        at = pl.ds(off // 4, n // 4)
        for k in (1, 3, 2):
            self.arrive(self.c.at[lax.rem(self.q[third] + 4 - k, 4), at], self.slot(2, s, k))
        block = self.out.at[self.quarter(s, self.q[first]), self.columns(self.q[second])]
        block[...] = (self.c[0, at, :] + self.c[1, at, :]) + (self.c[2, at, :] + self.c[3, at, :])
        for k, k2 in STEPS:
            self.start(block, block, self.plane(1, s, k, k2), peer(self.q, self.core, first, k, second, k2))

    def forward(self, s, ks):
        first, second = AXES[s][0], AXES[s][1]
        for k in ks:
            rows = self.quarter(s, lax.rem(self.q[first] + 4 - k, 4))
            for k2 in (0, 1, 3, 2):
                if k or k2:
                    block = self.out.at[rows, self.columns(lax.rem(self.q[second] + 4 - k2, 4))]
                    self.arrive(block, self.plane(1, s, k, k2))
            self.start(self.out.at[rows], self.out.at[rows], 49 + s * 4 + k, device(self.q, 1 - self.core))


STEPS = tuple((k, k2) for k in (2, 1, 3, 0) for k2 in (2, 1, 3, 0) if k or k2)


WIDE = ((0, 96), (96, 96), (192, 64))
SMALL = ((0, 64), (64, 64), (128, 64))


def project_kernel(scale, block_in, basis_in, ph_out, pl_out, gram, coeffs_out, bs, bk, sh, sl, kh, kl, ph, pl_, x1, coeffs, x2,
                   load, *rest):
    buffers0, buffers1, buffers2, store = rest[0:7], rest[7:14], rest[14:20], rest[20]
    q, core = position()
    loads = []
    for i in range(4):
        at = pl.ds(i * 256, 256)
        loads.append((pltpu.make_async_copy(basis_in.at[at], bs.at[at], load.at[0, i]),
                      pltpu.make_async_copy(block_in.at[at], bk.at[at], load.at[1, i])))
    for pair in loads:
        for copy in pair:
            copy.start()
    barrier = pltpu.get_barrier_semaphore()
    partners = [device(q, 1 - core)] + [peer(q, core, axis, k) for axis in range(3) for k in (1, 2, 3)]
    partners += [peer(q, core, first, k, second, k2) for first, second, _ in AXES for k in (1, 2, 3) for k2 in (1, 2, 3)]
    for to in partners:
        pl.semaphore_signal(barrier, inc=1, device_id=to, device_id_type=MESH)

    for i in range(4):
        for copy in loads[i]:
            copy.wait()

        @pl.loop(i * 2, i * 2 + 2)
        def _(j):
            at = pl.ds(pl.multiple_of(j * 128, 128), 128)
            hi, lo = split(bs[at, :])
            sh[at, :] = hi
            sl[at, :] = lo
            hi, lo = split(bk[at, :])
            kh[at, :] = hi
            kl[at, :] = lo

    def terms(at):
        columns = pl.ds(pl.multiple_of(at, 256), 256)
        x1[columns, :] = dot3(sh[:, columns], sl[:, columns], kh[...], kl[...], TN)

    sums = [Sum(256, 512, 256 * i, WIDE, x1, coeffs, *half) for i, half in enumerate((buffers0[:7], buffers1[:7]))]
    for i in range(2):
        terms((1 - core) * 512 + i * 256)
        if i == 0:
            pl.semaphore_wait(barrier, len(partners))
        sums[i].give()
    for i in range(2):
        terms(core * 512 + i * 256)
        sums[i].take()
        for s in range(3):
            sums[i].phase_a(s)
    for phase in ("phase_b", "phase_c", "phase_d", "phase_e"):
        for each in sums:
            for s in range(3):
                getattr(each, phase)(s)

    def subtract(at, last=False):
        rows = pl.ds(pl.multiple_of(at, 256), 256)
        hi, lo = split(coeffs[rows, :])
        kh[rows, :] = hi
        kl[rows, :] = lo

        @pl.loop(0, 4)
        def _(i):
            at = pl.ds(pl.multiple_of(i * 256, 256), 256)
            left = bk[at, :] - dot3(sh[at, rows], sl[at, rows], kh[rows, :], kl[rows, :], NN)
            if last:
                hi, lo = split(left)
                ph[at, :] = hi
                pl_[at, :] = lo
            else:
                bk[at, :] = left

    for i in range(2):
        for ks in ((1, 3), (2,)):
            for s in range(3):
                sums[i].phase_f(s, ks)
        subtract(core * 512 + i * 256)
    for i in range(2):
        sums[i].meet()
        subtract((1 - core) * 512 + i * 256, last=i == 1)

    keep = [pltpu.make_async_copy(coeffs, coeffs_out, store.at[0])]
    keep[0].start()

    keep += [pltpu.make_async_copy(ph, ph_out, store.at[1]), pltpu.make_async_copy(pl_, pl_out, store.at[2])]
    keep[1].start()
    keep[2].start()
    left = pl.ds(0, 256)
    right = pl.ds(256, 256)
    x2[0:256, :] = dot3(ph[:, left], pl_[:, left], ph[...], pl_[...], TN) * scale
    corner = dot3(ph[:, right], pl_[:, right], ph[:, right], pl_[:, right], TN) * scale
    x2[256:384, 0:256] = corner[0:128]
    x2[256:384, 256:512] = corner[128:256]
    halves, b, c, send, recv = buffers2[0], buffers2[1], buffers2[2], buffers2[3], buffers2[4]
    last = PlaneSum(192, 192, 0, SMALL, x2, gram, halves, None, None, b, c, send, recv)
    last.give()
    last.take()
    for phase in (last.scatter, last.exchange, last.gather):
        for s in range(3):
            phase(s)
    for ks in ((0, 1, 3), (2,)):
        for s in range(3):
            last.forward(s, ks)
    last.meet()
    for each in (*sums, last):
        each.drain()
    for copy in keep:
        copy.wait()


def buffers(half):
    return [
        pltpu.VMEM((half, 512), F32), pltpu.VMEM((3, half // 4, 512), F32), pltpu.VMEM((half // 4, 512), F32),
        pltpu.VMEM((3, half // 4, 128), F32), pltpu.VMEM((4, half // 4, 128), F32),
        pltpu.SemaphoreType.DMA((61,)), pltpu.SemaphoreType.DMA((61,)),
    ]


def project(block, basis, rows_total):
    anywhere = pl.BlockSpec(memory_space=pl.ANY)
    return pl.pallas_call(
        functools.partial(project_kernel, 1.0 / rows_total),
        out_shape=[
            jax.ShapeDtypeStruct((1024, 512), BF16), jax.ShapeDtypeStruct((1024, 512), BF16),
            jax.ShapeDtypeStruct((384, 512), F32), jax.ShapeDtypeStruct((1024, 512), F32),
        ],
        in_specs=[anywhere] * 2,
        out_specs=[anywhere, anywhere, pl.BlockSpec(memory_space=pltpu.VMEM), anywhere],
        scratch_shapes=[
            pltpu.VMEM((1024, 1024), F32), pltpu.VMEM((1024, 512), F32),
            pltpu.VMEM((1024, 1024), BF16), pltpu.VMEM((1024, 1024), BF16),
            pltpu.VMEM((1024, 512), BF16), pltpu.VMEM((1024, 512), BF16),
            pltpu.VMEM((1024, 512), BF16), pltpu.VMEM((1024, 512), BF16),
            pltpu.VMEM((1024, 512), F32), pltpu.VMEM((1024, 512), F32), pltpu.VMEM((384, 512), F32),
            pltpu.SemaphoreType.DMA((2, 4)),
            *buffers(256), *buffers(256),
            pltpu.VMEM((192, 512), F32), pltpu.VMEM((15, 48, 128), F32), pltpu.VMEM((4, 48, 128), F32),
            pltpu.SemaphoreType.DMA((151,)), pltpu.SemaphoreType.DMA((151,)), pltpu.SemaphoreType.DMA((1,)),
            pltpu.SemaphoreType.DMA((3,)),
        ],
        compiler_params=pltpu.CompilerParams(
            collective_id=0, has_side_effects=True, vmem_limit_bytes=48 * 2**20),
    )(block, basis)


def eliminate(t):
    sub = lax.broadcasted_iota(jnp.int32, (8, 128), 0)
    lane = lax.broadcasted_iota(jnp.int32, (8, 128), 1)

    def row(v, j):
        return jnp.broadcast_to(v[j : j + 1, :], (8, 128))

    def col(v, c):
        return jnp.broadcast_to(v[:, c : c + 1], (8, 128))

    def total(terms):
        while len(terms) > 1:
            terms = [terms[i] + terms[i + 1] for i in range(0, len(terms), 2)]
        return terms[0]

    def stack(v, order):
        h = v.astype(BF16).astype(F32)
        m = (v - h).astype(BF16).astype(F32)
        three = h, m, v - h - m
        return jnp.concatenate([three[i] for i in order], axis=0).astype(BF16)

    def solve(x, v0, v1, lo):
        x = x + [v0, v1]
        raw0, raw1 = v0, v1
        end = len(x)
        a_of = jnp.ones((8, 128), F32)
        b_of = d_of = jnp.zeros((8, 128), F32)
        for j in range(0, 8, 2):
            even, odd = sub == j, sub == j + 1
            pair = even | odd
            top = [row(v, j) if n > j else None for n, v in enumerate(x)]
            low = [row(v, j + 1) if n > j else None for n, v in enumerate(x)]
            a, b, c = row(x[j], j), top[j + 1], low[j + 1]
            g = 1.0 / (a * c - b * b)
            n0 = jnp.where(even, c, jnp.where(odd, -b, x[j + 1] * b - x[j] * c))
            n1 = jnp.where(even, -b, jnp.where(odd, a, x[j] * b - x[j + 1] * a))
            raw0 = jnp.where(even, top[end - 2], jnp.where(odd, low[end - 2], raw0))
            raw1 = jnp.where(even, top[end - 1], jnp.where(odd, low[end - 1], raw1))
            a_of = jnp.where(odd, a, a_of)
            b_of = jnp.where(odd, b, b_of)
            d_of = jnp.where(even, a, jnp.where(odd, c, d_of))
            for n in range(j + 2, end):
                x[n] = jnp.where(pair, 0.0, x[n]) + g * (n0 * top[n] + n1 * low[n])
        m = b_of / a_of
        q = 1.0 / jnp.sqrt(d_of - m * b_of)
        u0 = raw0 - m * pltpu.roll(raw0, 1, 0)
        u1 = raw1 - m * pltpu.roll(raw1, 1, 0)
        t[lo : lo + 8, 0:128] = jnp.where(lane >= sub + lo, u0 * q, 0.0)
        t[lo : lo + 8, 128:256] = u1 * q
        return x

    now = [(t[i : i + 8, 0:128], t[i : i + 8, 128:256]) for i in (0, 8)]
    for p in range(8):
        lo = 16 * p
        (a0, a1), (b0, b1) = now
        own = [col(a0, lo + k) for k in range(8)]
        across = [col(a0, lo + 8 + k) for k in range(8)]
        down = [col(b0, lo + k) for k in range(8)]
        corner = [col(b0, lo + 8 + k) for k in range(8)]
        x = solve(own + across, a0, a1, lo)
        across, y0, y1 = x[8:16], x[16], x[17]
        corner = [corner[k] - total([down[m] * row(across[k], m) for m in range(8)]) for k in range(8)]
        c0 = b0 - total([down[m] * row(y0, m) for m in range(8)])
        c1 = b1 - total([down[m] * row(y1, m) for m in range(8)])
        x = solve(corner, c0, c1, lo + 8)
        z0, z1 = x[8], x[9]
        if p == 7:
            break
        y0 = y0 - total([across[k] * row(z0, k) for k in range(8)])
        y1 = y1 - total([across[k] * row(z1, k) for k in range(8)])
        now = []
        for i in (lo + 16, lo + 24):
            v0, v1 = t[i : i + 8, 0:128], t[i : i + 8, 128:256]
            ci = [col(v0, lo + k) for k in range(16)]
            now.append((v0 - total([ci[k] * row((y0, z0)[k // 8], k % 8) for k in range(16)]),
                        v1 - total([ci[k] * row((y1, z1)[k // 8], k % 8) for k in range(16)])))
        if p < 6:
            left = stack(jnp.concatenate([a0, b0], axis=0), (0, 0, 1, 0, 2, 1))
            right = jnp.concatenate([jnp.concatenate([y0, y1], axis=1), jnp.concatenate([z0, z1], axis=1)], axis=0)
            change = lax.dot_general(left, stack(right, (0, 1, 0, 2, 0, 1)), (((0,), (0,)), ((), ())), preferred_element_type=F32)
            t[lo + 32 :, :] -= change[lo + 32 :, :]


SECOND = (0, 1, 0, 2, 0, 1)


def parts(v, order, axis):
    h = v.astype(BF16).astype(F32)
    m = (v - h).astype(BF16).astype(F32)
    three = [each.astype(BF16) for each in (h, m, v - h - m)]
    return jnp.concatenate([three[i] for i in order], axis=axis)


def factor_kernel(g, ph, pl_, coeffs, ortho_out, r_out, coeffs_out, ortho, r, s, t, w, root, sems):
    stores = [pltpu.make_async_copy(coeffs, coeffs_out, sems.at[0])]
    stores[0].start()
    n = 512
    zeros = jnp.zeros((128, 128), F32)
    for b in range(4):
        at = slice(b * 128, b * 128 + 128)
        for c in range(b):
            r[at, c * 128 : c * 128 + 128] = zeros
            s[at, n + c * 128 : n + c * 128 + 128] = zeros
        if b % 2 == 0:
            w[at, b * 128 + 128 : b * 128 + 256] = zeros
    eye = lax.broadcasted_iota(jnp.int32, (128, 128), 0) == lax.broadcasted_iota(jnp.int32, (128, 128), 1)
    s[0:256, 0:n] = g[0:256, :]
    s[256:384, 256:n] = g[256:384, 0:256]
    s[384:512, 256:n] = g[256:384, 256:n]
    down = []
    for b in range(4):
        at = slice(b * 128, b * 128 + 128)
        diagonal = jnp.where(eye, s[at, at], 0.0)
        across = jnp.sqrt(jnp.sum(diagonal, axis=0, keepdims=True))
        root[0:1, at] = across
        root[1:2, at] = 1.0 / across
        s[at, n + b * 128 : n + b * 128 + 128] = jnp.where(eye, 1.0 / across, 0.0)
        down.append(1.0 / jnp.sqrt(jnp.sum(diagonal, axis=1, keepdims=True)))
    for b in range(4):
        at = slice(b * 128, b * 128 + 128)
        s[at, b * 128 : n] = s[at, b * 128 : n] * down[b] * root[1:2, b * 128 : n]

    def body(step, carry):
        for b in range(4):
            @pl.when(step == b)
            def _():
                t[:, 0:128] = s[b * 128 : b * 128 + 128, b * 128 : b * 128 + 128]
                t[:, 128:256] = s[b * 128 : b * 128 + 128, n + b * 128 : n + b * 128 + 128]
        eliminate(t)
        for b in range(4):
            @pl.when(step == b)
            def _():
                lo, hi = b * 128, b * 128 + 128
                scaled = t[:, 128:256]
                li = scaled * root[0:1, lo:hi]
                r[lo:hi, lo:hi] = t[:, 0:128] * root[0:1, lo:hi]
                w[lo:hi, lo:hi] = scaled
                left = parts(li, (0, 0, 1, 0, 2, 1), 1)
                if b:
                    w[lo:hi, 0:lo] = dot(left, parts(s[lo:hi, n : n + lo], SECOND, 0), NN)
                if b < 3:
                    right = dot(left, parts(s[lo:hi, hi:n], SECOND, 0), NN)
                    r[lo:hi, hi:n] = right * root[0:1, hi:n]
                    down = parts(right, (0, 0, 1, 0, 2, 1), 0)
                    across = parts(right, SECOND, 0)
                    inverse = parts(w[lo:hi, 0:hi], SECOND, 0)
                    for c in range(b + 1, 4):
                        at = slice(c * 128, c * 128 + 128)
                        first = (c - b - 1) * 128
                        rows = down[:, first : first + 128]
                        s[at, c * 128 : n] -= dot(rows, across[:, first:], TN)
                        s[at, n : n + hi] -= dot(rows, inverse, TN)
        return carry

    lax.fori_loop(0, 4, body, 0)
    stores.append(pltpu.make_async_copy(r, r_out, sems.at[1]))
    stores[1].start()
    halves = [split(w[c * 256 : c * 256 + 256, 0 : c * 256 + 256]) for c in range(2)]
    for i in range(4):
        rows = slice(i * 256, i * 256 + 256)
        for c in range(2):
            at, k = slice(c * 256, c * 256 + 256), slice(0, c * 256 + 256)
            ortho[rows, at] = dot3(ph[rows, k], pl_[rows, k], *halves[c], NT)
        stores.append(pltpu.make_async_copy(ortho.at[pl.ds(i * 256, 256)], ortho_out.at[pl.ds(i * 256, 256)], sems.at[2 + i]))
        stores[-1].start()
    for copy in stores:
        copy.wait()


def orthogonalize(gram, ph, pl_, coeffs):
    anywhere = pl.BlockSpec(memory_space=pl.ANY)
    return pl.pallas_call(
        factor_kernel,
        out_shape=[
            jax.ShapeDtypeStruct((1024, 512), F32), jax.ShapeDtypeStruct((512, 512), F32),
            jax.ShapeDtypeStruct((1024, 512), F32),
        ],
        in_specs=[pl.BlockSpec(memory_space=pltpu.VMEM)] * 3 + [anywhere],
        out_specs=[anywhere] * 3,
        scratch_shapes=[
            pltpu.VMEM((1024, 512), F32), pltpu.VMEM((512, 512), F32),
            pltpu.VMEM((512, 1024), F32), pltpu.VMEM((128, 256), F32), pltpu.VMEM((512, 512), F32),
            pltpu.VMEM((8, 512), F32), pltpu.SemaphoreType.DMA((6,)),
        ],
        compiler_params=pltpu.CompilerParams(vmem_limit_bytes=40 * 2**20),
    )(gram, ph, pl_, coeffs)


def shards(block, basis):
    rows_total = block.shape[0] * lax.axis_size("leaf") * lax.axis_size("side")
    ph, pl_, gram, coeffs = project(block, basis, rows_total)
    return orthogonalize(gram, ph, pl_, coeffs)


def solution(mesh):
    return jax.shard_map(
        shards,
        mesh=mesh,
        in_specs=(P(("leaf", "side"), None), P(("leaf", "side"), None)),
        out_specs=(P(("leaf", "side"), None), P(), P()),
        check_vma=False,
    )
```
